32 devices in a mesh: sec: 4 (over y, x), tile: 8 (over z, core).
Axes of the slice: x: 2, y: 2, z: 4, core: 2. Of those that a mesh axis runs over, the one named last changes fastest.
Arguments:
- pan_source: bfloat16 [32, 256, 384], P(('sec', 'tile'))
- ms_source: bfloat16 [8, 32, 64, 96], P(None, ('sec', 'tile'))
- row_tap: int32 [32, 256], P(('sec', 'tile')), may hold values from 0 to 316, as said below
- row_frac: float32 [32, 256], P(('sec', 'tile')), may hold values from 0 to 1
- col_tap: int32 [32, 384], P(('sec', 'tile')), may hold values from 0 to 444, as said below
- col_frac: float32 [32, 384], P(('sec', 'tile')), may hold values from 0 to 1
- ms_row_tap: int32 [32, 256], P(('sec', 'tile')), may hold values from 0 to 76, as said below
- ms_row_frac: float32 [32, 256], P(('sec', 'tile')), may hold values from 0 to 1
- ms_col_tap: int32 [32, 384], P(('sec', 'tile')), may hold values from 0 to 108, as said below
- ms_col_frac: float32 [32, 384], P(('sec', 'tile')), may hold values from 0 to 1
Outputs:
- ms_sharp: bfloat16 [8, 32, 256, 384], P(None, ('sec', 'tile'))
The draws below stay inside these ranges and needn't reach their ends.
Inputs may be any that keep to these rules, and one draw needn't show every extreme that they name: Each row of row_tap starts at 0 and rises by 0, 1 or 2 from one map row to the next. Each row of col_tap starts at 0 and rises by 0, 1 or 2 from one map column to the next. Each row of ms_row_tap starts at 0 and rises by 0 or 1 from one map row to the next. Each row of ms_col_tap starts at 0 and rises by 0 or 1 from one map column to the next.
All inputs are finite; a program needn't handle non-finite values.
Results may differ from the reference program's by a relative error of at most 0.0045.
Values may be sent and summed in bfloat16 or wider, within the bound.
A program may use at most 128 MiB of HBM per device.

```python
import math
import jax
import jax.numpy as jnp
from jax import lax

BANDS = 8
TR = 256
TC = 384
MR = 64
MC = 96
HALO = 32
MHALO = 8
RADIUS = 8
NT = 32


def sensor_fields(key):
    keys_all = jax.random.split(jax.random.fold_in(key, 5), 9)
    coarse = jnp.clip(jax.random.normal(keys_all[0], (NT, MR, MC), jnp.float32), -4.0, 4.0)
    fine = jnp.clip(jax.random.normal(keys_all[1], (NT, TR, TC), jnp.float32), -4.0, 4.0)
    ms_noise = jnp.clip(jax.random.normal(keys_all[2], (BANDS, NT, MR, MC), jnp.float32), -4.0, 4.0)
    bright_share = 1.0 / 12.0
    bright_low = 2.5
    bright_high = 4.0
    darker_low = 0.35
    darker_high = 1.0
    mixing = jax.random.uniform(keys_all[4], (BANDS, 1, 1, 1), jnp.float32, 0.3, 0.9)
    upsampled = jnp.repeat(jnp.repeat(coarse, 4, axis=1), 4, axis=2)
    pan = 0.6 * upsampled + 0.8 * fine
    row_scale = jnp.exp(jax.random.uniform(keys_all[5], (NT, TR, 1), jnp.float32, math.log(0.5), math.log(2.0)))
    column_keys = jax.random.split(keys_all[6], 3)
    chooser = jax.random.uniform(column_keys[0], (NT, 1, TC), jnp.float32, 0.0, 1.0)
    bright = jnp.exp(jax.random.uniform(column_keys[1], (NT, 1, TC), jnp.float32, math.log(bright_low), math.log(bright_high)))
    darker = jnp.exp(jax.random.uniform(column_keys[2], (NT, 1, TC), jnp.float32, math.log(darker_low), math.log(darker_high)))
    col_scale = jnp.where(chooser < bright_share, bright, darker)
    pan = pan * row_scale * col_scale
    bands = mixing * coarse[None] + jnp.sqrt(1.0 - mixing * mixing) * ms_noise
    ms_row_scale = jnp.exp(jax.random.uniform(keys_all[7], (1, NT, MR, 1), jnp.float32, math.log(0.5), math.log(2.0)))
    ms_col_scale = jnp.exp(jax.random.uniform(keys_all[8], (1, NT, 1, MC), jnp.float32, math.log(0.5), math.log(2.0)))
    bands = bands * ms_row_scale * ms_col_scale
    return (pan, bands)


def draw_pan_source(key, part):
    pan, bands = sensor_fields(key)
    return pan.astype(jnp.bfloat16)


def draw_ms_source(key, part):
    pan, bands = sensor_fields(key)
    return bands.astype(jnp.bfloat16)


def tap_table(key, count, length, margin):
    zeros_count = length // 8
    twos_count = 2 * margin - 3 + zeros_count
    keys_all = jax.random.split(key, count)

    def one_row(row_key):
        shuffled = jax.random.permutation(row_key, length - 1)
        increments = jnp.where(shuffled < zeros_count, 0, jnp.where(shuffled < zeros_count + twos_count, 2, 1)).astype(jnp.int32)
        return jnp.concatenate([jnp.zeros((1,), jnp.int32), jnp.cumsum(increments).astype(jnp.int32)])
    return jax.vmap(one_row)(keys_all)


def coarse_table(key, count, length, rise_total):
    keys_all = jax.random.split(key, count)

    def one_row(row_key):
        shuffled = jax.random.permutation(row_key, length - 1)
        increments = jnp.where(shuffled < rise_total, 1, 0).astype(jnp.int32)
        return jnp.concatenate([jnp.zeros((1,), jnp.int32), jnp.cumsum(increments).astype(jnp.int32)])
    return jax.vmap(one_row)(keys_all)


def draw_row_tap(key, part):
    return tap_table(jax.random.fold_in(key, 11), NT, TR, HALO)


def draw_col_tap(key, part):
    return tap_table(jax.random.fold_in(key, 23), NT, TC, HALO)


def draw_ms_row_tap(key, part):
    return coarse_table(jax.random.fold_in(key, 37), NT, TR, MR + 2 * MHALO - 4)


def draw_ms_col_tap(key, part):
    return coarse_table(jax.random.fold_in(key, 41), NT, TC, MC + 2 * MHALO - 4)


def block_levels(stream_key, dims, cuts, least, high):
    def one(position, blocks):
        draws = jax.random.uniform(jax.random.fold_in(jax.random.fold_in(stream_key, 6), position), (blocks,), jnp.float32, least / len(cuts), high / len(cuts))
        return jnp.repeat(jnp.exp(draws), dims[position] // blocks).reshape((-1,) + (1,) * (len(dims) - position - 1))

    loudness = one(*cuts[0])
    for cut in cuts[1:]:
        loudness = loudness * one(*cut)
    return loudness


def setup_inputs(seed: int = 0) -> dict:
    key_list = jax.random.split(jax.random.key(seed), 11)
    return {
        "pan_source": draw_pan_source(jax.random.fold_in(key_list[10], 71), 0),
        "ms_source": draw_ms_source(jax.random.fold_in(key_list[10], 71), 0),
        "row_tap": draw_row_tap(jax.random.fold_in(key_list[10], 71), 0),
        "row_frac": jnp.clip(1.0 * jax.random.uniform(key_list[3], (NT, TR), jnp.float32) ** block_levels(key_list[3], (NT, TR), ((0, 32),), -0.2, 0.2), 0.0, 1.0),
        "col_tap": draw_col_tap(jax.random.fold_in(key_list[10], 71), 0),
        "col_frac": jnp.clip(1.0 * jax.random.uniform(key_list[5], (NT, TC), jnp.float32) ** block_levels(key_list[5], (NT, TC), ((0, 32),), -0.2, 0.2), 0.0, 1.0),
        "ms_row_tap": draw_ms_row_tap(jax.random.fold_in(key_list[10], 71), 0),
        "ms_row_frac": jnp.clip(1.0 * jax.random.uniform(key_list[7], (NT, TR), jnp.float32) ** block_levels(key_list[7], (NT, TR), ((0, 32),), -0.2, 0.2), 0.0, 1.0),
        "ms_col_tap": draw_ms_col_tap(jax.random.fold_in(key_list[10], 71), 0),
        "ms_col_frac": jnp.clip(1.0 * jax.random.uniform(key_list[9], (NT, TC), jnp.float32) ** block_levels(key_list[9], (NT, TC), ((0, 32),), -0.2, 0.2), 0.0, 1.0),
    }


EPSILON = 0.1


def cubic_weights(fraction):
    linear = fraction.astype(jnp.float32)
    squared = linear * linear
    cubed = squared * linear
    return jnp.stack([-0.5 * cubed + squared - 0.5 * linear,
                      1.5 * cubed - 2.5 * squared + 1.0,
                      -1.5 * cubed + 2.0 * squared + 0.5 * linear,
                      0.5 * cubed - 0.5 * squared], axis=0)


def rounded(values):
    return lax.optimization_barrier(values.astype(jnp.bfloat16)).astype(jnp.float32)


def window_sum(values, along_axis, window):
    total_length = values.shape[along_axis]
    kept_length = total_length - window + 1
    result = None
    partial_value = values
    stride = 1
    begin_at = 0
    while stride <= window:
        if window & stride:
            addend = lax.slice_in_dim(partial_value, begin_at, begin_at + kept_length, axis=along_axis)
            result = addend if result is None else result + addend
            begin_at = begin_at + stride
        if stride * 2 <= window:
            extent = partial_value.shape[along_axis]
            partial_value = lax.slice_in_dim(partial_value, 0, extent - stride, axis=along_axis) + lax.slice_in_dim(partial_value, stride, extent, axis=along_axis)
        stride = stride * 2
    return result


def coverage(anchor, amount, extent, radius):
    places = anchor + lax.iota(jnp.int32, amount)
    highest = jnp.minimum(places + radius, extent - 1)
    lowest = jnp.maximum(places - radius, 0)
    return (highest - lowest + 1).astype(jnp.float32)


def resample_all(stack, first_rows, row_fracs, first_cols, col_fracs, margin, out_rows, out_cols):
    channels = stack.shape[0]
    tiles_all = stack.shape[1]
    tile_rows = stack.shape[2]
    tile_cols = stack.shape[3]
    grid_rows = tiles_all // 4
    sensor_map = stack.reshape(channels, grid_rows, 4, tile_rows, tile_cols).transpose(0, 1, 3, 2, 4).reshape(channels, grid_rows * tile_rows, 4 * tile_cols)
    padded = jnp.pad(sensor_map, ((0, 0), (margin, margin), (margin, margin)))

    def one_tile(tile):
        anchor_row = ((tile // 4) * tile_rows).astype(jnp.int32)
        anchor_col = ((tile % 4) * tile_cols).astype(jnp.int32)
        patch_block = lax.dynamic_slice(padded, (jnp.int32(0), anchor_row, anchor_col), (channels, tile_rows + 2 * margin, tile_cols + 2 * margin)).astype(jnp.float32)
        row_weights = rounded(cubic_weights(row_fracs[tile]))
        col_weights = rounded(cubic_weights(col_fracs[tile]))
        row_first = first_rows[tile].astype(jnp.int32)
        col_first = first_cols[tile].astype(jnp.int32)
        row_segment = jnp.zeros((channels, out_rows, tile_cols + 2 * margin), jnp.float32)
        for tap_shift in range(4):
            row_segment = row_segment + patch_block[:, row_first + tap_shift, :] * row_weights[tap_shift][None, :, None]
        row_segment = rounded(row_segment)
        result = jnp.zeros((channels, out_rows, out_cols), jnp.float32)
        for tap_shift in range(4):
            result = result + row_segment[:, :, col_first + tap_shift] * col_weights[tap_shift][None, None, :]
        return result.astype(jnp.bfloat16)

    return lax.map(one_tile, jnp.arange(tiles_all, dtype=jnp.int32))


def reference(pan_source, ms_source, row_tap, row_frac, col_tap, col_frac, ms_row_tap, ms_row_frac, ms_col_tap, ms_col_frac):
    pan_source = jnp.roll(pan_source, 2, axis=0)
    ms_source = jnp.roll(ms_source, 2, axis=1)
    row_tap = jnp.roll(row_tap, 2, axis=0)
    row_frac = jnp.roll(row_frac, 2, axis=0)
    col_tap = jnp.roll(col_tap, 2, axis=0)
    col_frac = jnp.roll(col_frac, 2, axis=0)
    ms_row_tap = jnp.roll(ms_row_tap, 2, axis=0)
    ms_row_frac = jnp.roll(ms_row_frac, 2, axis=0)
    ms_col_tap = jnp.roll(ms_col_tap, 2, axis=0)
    ms_col_frac = jnp.roll(ms_col_frac, 2, axis=0)
    tiles_all = pan_source.shape[0]
    tile_rows = pan_source.shape[1]
    tile_cols = pan_source.shape[2]
    grid_rows = tiles_all // 4
    map_rows = grid_rows * tile_rows
    map_cols = 4 * tile_cols
    pan_tiles = resample_all(pan_source[None], row_tap, row_frac, col_tap, col_frac, HALO, tile_rows, tile_cols)
    ms_tiles = resample_all(ms_source, ms_row_tap, ms_row_frac, ms_col_tap, ms_col_frac, MHALO, tile_rows, tile_cols)
    tiles = jnp.concatenate([pan_tiles, ms_tiles], axis=1)
    channels = tiles.shape[1]
    resampled = tiles.reshape(grid_rows, 4, channels, tile_rows, tile_cols).transpose(2, 0, 3, 1, 4).reshape(channels, map_rows, map_cols)
    window = 2 * RADIUS + 1

    def box(values):
        widened = jnp.pad(values, ((RADIUS, RADIUS), (RADIUS, RADIUS)))
        return window_sum(window_sum(widened, 0, window), 1, window)

    row_cover = coverage(jnp.int32(0), map_rows, map_rows, RADIUS)
    col_cover = coverage(jnp.int32(0), map_cols, map_cols, RADIUS)
    coverage_map = row_cover[:, None] * col_cover[None, :]
    guide_image = resampled[0].astype(jnp.float32)
    mean_guide = box(guide_image) / coverage_map
    mean_square = box(guide_image * guide_image) / coverage_map
    variance = mean_square - mean_guide * mean_guide

    def one_band(band_image):
        values = band_image.astype(jnp.float32)
        mean_band = box(values) / coverage_map
        mean_cross = box(guide_image * values) / coverage_map
        gain_map = (mean_cross - mean_guide * mean_band) / (variance + EPSILON)
        offset_map = mean_band - gain_map * mean_guide
        gain_map = rounded(gain_map)
        offset_map = rounded(offset_map)
        return (box(gain_map) / coverage_map * guide_image + box(offset_map) / coverage_map).astype(jnp.bfloat16)

    sharpened = lax.map(one_band, resampled[1:])
    bands = sharpened.shape[0]
    placed = sharpened.reshape(bands, grid_rows, tile_rows, 4, tile_cols).transpose(0, 1, 3, 2, 4).reshape(bands, tiles_all, tile_rows, tile_cols)
    return jnp.roll(placed, -2, axis=1)
```

```python
import functools

import jax
import jax.numpy as jnp
from jax import lax
from jax.experimental import pallas as pl
from jax.experimental.pallas import tpu as pltpu
from jax.sharding import PartitionSpec as P

HALO = 32
MHALO = 8
RADIUS = 8
EPSILON = 0.1
GRID_COLS = 4
EDGE = 2 * RADIUS
LANES = 128
HALF = 256
GROUPS = 8
NOWHERE = -1000
MESH = pl.DeviceIdType.MESH

STEPS = ((1, 0), (-1, 0), (0, 1), (0, -1), (1, 1), (1, -1), (-1, 1), (-1, -1))


def cubic_weights(fraction):
    squared = fraction * fraction
    cubed = squared * fraction
    return (
        -0.5 * cubed + squared - 0.5 * fraction,
        1.5 * cubed - 2.5 * squared + 1.0,
        -1.5 * cubed + 2.0 * squared + 0.5 * fraction,
        0.5 * cubed - 0.5 * squared,
    )


def band(taps, fraction, length, shift):
    line = lax.broadcasted_iota(jnp.int32, (length, taps.shape[1]), 0)
    return band_at(line - shift, taps, fraction)


def band_at(position, taps, fraction):
    weights = cubic_weights(fraction)
    distance = position - taps
    matrix = jnp.zeros(position.shape, jnp.float32)
    for offset in range(4):
        matrix = jnp.where(distance == offset, weights[offset], matrix)
    return matrix.astype(jnp.bfloat16)


def spread(values, fill):
    lane = lax.broadcasted_iota(jnp.int32, (1, 2 * HALF), 1)
    both = jnp.concatenate([values[:, :HALF], values[:, values.shape[1] - HALF :]], axis=1)
    return jnp.where((lane >= HALF - EDGE) & (lane < HALF + EDGE), fill, both).astype(values.dtype)


def picker(shape, shift, low, high):
    source = lax.broadcasted_iota(jnp.int32, shape, 0)
    target = lax.broadcasted_iota(jnp.int32, shape, 1)
    chosen = (target - source == shift) & (source >= low) & (source < high)
    return jnp.where(chosen, 1.0, 0.0).astype(jnp.bfloat16)


def dot(left, right):
    return jnp.dot(left, right, preferred_element_type=jnp.float32)


def dot_t(left, right):
    return lax.dot_general(
        left, right, (((0,), (0,)), ((), ())), preferred_element_type=jnp.float32
    )


def place(sec_count, tile_count):
    total = sec_count * tile_count
    me = lax.axis_index("sec") * tile_count + lax.axis_index("tile")
    return lax.rem(me + 2, total), total


def resample_kernel(
    sec_count,
    tile_count,
    pan,
    ms,
    row_tap,
    row_frac,
    col_tap,
    col_frac,
    ms_row_tap,
    ms_row_frac,
    ms_col_tap,
    ms_col_frac,
    wide,
    ms_own,
    row_tap_here,
    row_frac_here,
    col_tap_here,
    col_frac_here,
    ms_row_tap_here,
    ms_row_frac_here,
    ms_col_tap_here,
    ms_col_frac_here,
    far_tap,
    far_frac,
    seg_edge,
    seg_got,
    side_edge,
    side_got,
    pan_patch,
    ms_vert,
    ms_tall,
    pan_pack,
    pan_got,
    ms_pack,
    ms_got,
    pack_east,
    pack_west,
    got_west,
    got_east,
    local_sem,
    table_sem,
    send_pan,
    recv_pan,
    send_ms,
    recv_ms,
    send_tall,
    recv_tall,
    send_table,
    recv_table,
):
    rows, cols = pan.shape
    bands, ms_rows, ms_cols = ms.shape
    placed, total = place(sec_count, tile_count)
    column = lax.rem(placed, GRID_COLS)
    grid_row = placed // GRID_COLS
    north_ok = grid_row > 0
    south_ok = grid_row < total // GRID_COLS - 1
    west_ok = column > 0
    east_ok = column < GRID_COLS - 1

    def device(down, right):
        there = lax.rem(placed + down * GRID_COLS + right - 2 + 2 * total, total)
        return (there // tile_count, lax.rem(there, tile_count))

    def reaches(down, right):
        ok = True
        if down:
            ok = south_ok if down > 0 else north_ok
        if right:
            side = east_ok if right > 0 else west_ok
            ok = side if ok is True else ok & side
        return ok

    def start_all(steps, copies):
        for (down, right), copy in zip(steps, copies):
            pl.when(reaches(down, right))(copy.start)

    def wait_all(steps, copies):
        for (down, right), copy in zip(steps, copies):
            pl.when(reaches(-down, -right))(copy.wait_recv)
        for (down, right), copy in zip(steps, copies):
            pl.when(reaches(down, right))(copy.wait_send)

    barrier = pltpu.get_barrier_semaphore()
    for down, right in STEPS:

        @pl.when(reaches(down, right))
        def _(down=down, right=right):
            pl.semaphore_signal(
                barrier, inc=1, device_id=device(down, right), device_id_type=MESH
            )

    own = pltpu.make_async_copy(
        pan, pan_patch.at[HALO : HALO + rows, LANES : LANES + cols], local_sem
    )
    fetched = [
        pltpu.make_async_copy(source, target, table_sem.at[index])
        for index, (source, target) in enumerate(
            (
                (row_tap, row_tap_here),
                (row_frac, row_frac_here),
                (col_tap, col_tap_here),
                (col_frac, col_frac_here),
                (ms_row_tap, ms_row_tap_here),
                (ms_row_frac, ms_row_frac_here),
                (ms_col_tap, ms_col_tap_here),
                (ms_col_frac, ms_col_frac_here),
                (ms, ms_own),
            )
        )
    ]
    for copy in fetched:
        copy.start()
    own.start()
    for copy in fetched:
        copy.wait()
    own.wait()
    group = rows // (LANES // HALO)
    ms_slot = LANES // 2
    for side in range(2):
        total_pan = jnp.zeros((group, LANES), jnp.float32)
        first_lane = 0 if side else LANES - HALO
        block = slice(LANES, 2 * LANES) if side else slice(cols, cols + LANES)
        for g in range(LANES // HALO):
            move = picker(
                (LANES, LANES), g * HALO - first_lane, first_lane, first_lane + HALO
            )
            lines = slice(HALO + g * group, HALO + (g + 1) * group)
            total_pan = total_pan + dot(pan_patch[lines, block], move)
        pan_pack[side] = total_pan.astype(jnp.bfloat16)
        total_ms = jnp.zeros((ms_rows, LANES), jnp.float32)
        first_lane = 0 if side else ms_cols - MHALO
        for b in range(bands):
            move = picker(
                (ms_cols, LANES),
                side * ms_slot + b * MHALO - first_lane,
                first_lane,
                first_lane + MHALO,
            )
            total_ms = total_ms + dot(ms_own[b], move)
        ms_pack[side] = total_ms.astype(jnp.bfloat16)
        lines = slice(0, MHALO) if side else slice(ms_rows - MHALO, ms_rows)
        for pair in range(bands // 2):
            both = [ms_own[b].astype(jnp.float32)[lines] for b in (2 * pair, 2 * pair + 1)]
            ms_tall[side, pair] = jnp.concatenate(both, axis=0).astype(jnp.bfloat16)

    tall = 1 + north_ok.astype(jnp.int32) + south_ok.astype(jnp.int32)
    broad = 1 + west_ok.astype(jnp.int32) + east_ok.astype(jnp.int32)
    pl.semaphore_wait(barrier, tall * broad - 1)

    def span(step, size, depth):
        if step > 0:
            return slice(size - depth, size), slice(0, depth)
        if step < 0:
            return slice(0, depth), slice(depth + size, 2 * depth + size)
        return slice(0, size), slice(depth, depth + size)

    steps, copies = [], []
    for index, (down, right) in enumerate(STEPS):
        row_from, row_to = span(down, rows, HALO)
        col_from, col_to = span(right, cols, LANES)
        side = 0 if right > 0 else 1
        if down:
            source, target = pan.at[row_from, col_from], pan_patch.at[row_to, col_to]
        else:
            source, target = pan_pack.at[side], pan_got.at[side]
        steps.append((down, right))
        copies.append(
            pltpu.make_async_remote_copy(
                src_ref=source,
                dst_ref=target,
                send_sem=send_pan.at[index],
                recv_sem=recv_pan.at[index],
                device_id=device(down, right),
                device_id_type=MESH,
            )
        )
        row_from, row_to = span(down, ms_rows, 16)
        if right:
            source, target = ms_pack.at[side, row_from, :], ms_got.at[side, row_to, :]
        else:
            source, target = ms_tall.at[0 if down > 0 else 1], ms_vert.at[0 if down > 0 else 1]
        steps.append((down, right))
        copies.append(
            pltpu.make_async_remote_copy(
                src_ref=source,
                dst_ref=target,
                send_sem=send_ms.at[index],
                recv_sem=recv_ms.at[index],
                device_id=device(down, right),
                device_id_type=MESH,
            )
        )
    for index, down in enumerate((1, -1)):
        for which, (source, target) in enumerate(((ms_col_tap, far_tap), (ms_col_frac, far_frac))):
            steps.append((down, 0))
            copies.append(
                pltpu.make_async_remote_copy(
                    src_ref=source,
                    dst_ref=target.at[index],
                    send_sem=send_table.at[2 * index + which],
                    recv_sem=recv_table.at[2 * index + which],
                    device_id=device(down, 0),
                    device_id_type=MESH,
                )
            )
    start_all(steps, copies)
    row_matrix = band(row_tap_here[...], row_frac_here[...], 2 * HALO + rows, 0)
    col_matrix = band(
        spread(col_tap_here[...], NOWHERE), spread(col_frac_here[...], 0), 2 * LANES + cols, LANES - HALO
    )
    ms_row_taps = ms_row_tap_here[...]
    ms_row_fracs = ms_row_frac_here[...]
    ms_row_matrix = band(ms_row_taps, ms_row_fracs, 32 + ms_rows, 16 - MHALO)
    line = lax.broadcasted_iota(jnp.int32, (32 + ms_rows, rows), 0)
    below = 16 + ms_rows
    away = -LANES
    first_of_pair = jnp.where(
        line < MHALO, line, jnp.where((line < 16) | (line >= below + MHALO), away, line - MHALO)
    )
    second_of_pair = jnp.where(
        line < MHALO,
        away,
        jnp.where(
            line < below, line - MHALO, jnp.where(line < below + MHALO, away, line - 2 * MHALO)
        ),
    )
    ms_pair_matrices = tuple(
        band_at(position, ms_row_taps, ms_row_fracs)
        for position in (first_of_pair, second_of_pair)
    )

    def ms_col_matrices(taps, fracs):
        taps, fracs = spread(taps, NOWHERE), spread(fracs, 0)
        lane = lax.broadcasted_iota(jnp.int32, (LANES, taps.shape[1]), 0)
        position = jnp.where(lane < ms_slot, 0, ms_cols + MHALO) + (lane & (MHALO - 1))
        return band(taps, fracs, ms_cols, -MHALO), band_at(position, taps, fracs)

    ms_own_matrix, ms_halo_matrix = ms_col_matrices(ms_col_tap_here[...], ms_col_frac_here[...])
    packers = []
    for shift in (LANES - EDGE, 0):
        line = lax.broadcasted_iota(jnp.int32, (GROUPS * LANES, LANES), 0)
        lane = lax.broadcasted_iota(jnp.int32, (GROUPS * LANES, LANES), 1)
        place_in = (line & (LANES - 1)) - shift
        good = (place_in >= 0) & (place_in < EDGE) & (lane == (line // LANES) * EDGE + place_in)
        packers.append(jnp.where(good, 1.0, 0.0).astype(jnp.bfloat16))

    wait_all(steps, copies)

    def clear(ok, ref):
        @pl.when(jnp.logical_not(ok))
        def _():
            ref[...] = jnp.zeros(ref.shape, ref.dtype)

    clear(west_ok, pan_got.at[0])
    clear(east_ok, pan_got.at[1])
    for side in range(2):
        first_lane = 0 if side else LANES - HALO
        block = slice(LANES + cols, 2 * LANES + cols) if side else slice(0, LANES)
        for g in range(LANES // HALO):
            move = picker((LANES, LANES), first_lane - g * HALO, g * HALO, (g + 1) * HALO)
            lines = slice(HALO + g * group, HALO + (g + 1) * group)
            pan_patch[lines, block] = dot(pan_got[side], move).astype(jnp.bfloat16)

    clear(north_ok, pan_patch.at[:HALO, :])
    clear(south_ok, pan_patch.at[HALO + rows :, :])
    clear(west_ok, pan_patch.at[:, :LANES])
    clear(east_ok, pan_patch.at[:, LANES + cols :])
    clear(north_ok, ms_vert.at[0])
    clear(south_ok, ms_vert.at[1])
    for side, ok in ((0, west_ok), (1, east_ok)):
        clear(ok, ms_got.at[side])
        clear(north_ok, ms_got.at[side, :16, :])
        clear(south_ok, ms_got.at[side, 16 + ms_rows :, :])

    tall_steps, tall_copies = [], []

    def send(down, right, source, target):
        index = len(tall_copies)
        tall_steps.append((down, right))
        tall_copies.append(
            pltpu.make_async_remote_copy(
                src_ref=source,
                dst_ref=target,
                send_sem=send_tall.at[index],
                recv_sem=recv_tall.at[index],
                device_id=device(down, right),
                device_id_type=MESH,
            )
        )
        start_all(tall_steps[-1:], tall_copies[-1:])

    mid = slice(EDGE, EDGE + rows)
    ends = (slice(rows - EDGE, rows), slice(0, EDGE))
    segment = dot_t(row_matrix, pan_patch[...]).astype(jnp.bfloat16)
    wide[0, mid, :] = dot(segment, col_matrix).astype(jnp.bfloat16)
    send(1, 0, wide.at[0, rows : rows + EDGE], wide.at[0, :EDGE])
    send(-1, 0, wide.at[0, EDGE : 2 * EDGE], wide.at[0, EDGE + rows :])
    lane = lax.broadcasted_iota(jnp.int32, (rows, LANES), 1)
    halo_segment = dot_t(ms_row_matrix, ms_got[0]) + dot_t(ms_row_matrix, ms_got[1])
    for end in range(2):
        side_edge[end] = halo_segment[ends[end]].astype(jnp.bfloat16)
        send(1 - 2 * end, 0, side_edge.at[end], side_got.at[end])
    halo_band = (lane & (ms_slot - 1)) // MHALO
    for b in range(bands):
        block = jnp.concatenate([ms_vert[0, b // 2], ms_own[b], ms_vert[1, b // 2]], axis=0)
        segment = dot_t(ms_pair_matrices[b % 2], block).astype(jnp.bfloat16)
        for end in range(2):
            seg_edge[end, b] = segment[ends[end]]
        beside = jnp.where(halo_band == b, halo_segment, 0.0).astype(jnp.bfloat16)
        wide[b + 1, mid, :] = (
            dot(segment, ms_own_matrix) + dot(beside, ms_halo_matrix)
        ).astype(jnp.bfloat16)
        if b % 4 == 3:
            for end in range(2):
                part = slice(b - 3, b + 1)
                send(1 - 2 * end, 0, seg_edge.at[end, part], seg_got.at[end, part])

    depth = rows // GROUPS
    for pack, block, packer in (
        (pack_east, slice(wide.shape[2] - LANES, wide.shape[2]), packers[0]),
        (pack_west, slice(0, LANES), packers[1]),
    ):
        fields = [wide[b + 1, mid, block] for b in range(bands)]
        pack[:rows] = dot(jnp.concatenate(fields, axis=1), packer).astype(jnp.bfloat16)
        fields = [
            wide[0, EDGE + g * depth : EDGE + (g + 1) * depth, block] for g in range(GROUPS)
        ]
        pack[rows:] = dot(jnp.concatenate(fields, axis=1), packer).astype(jnp.bfloat16)
    south_ms = EDGE + rows + depth
    north_pan = south_ms + EDGE
    south_pan = north_pan + EDGE
    for right, source, target in ((1, pack_east, got_west), (-1, pack_west, got_east)):
        send(0, right, source, target.at[EDGE:south_ms])
        send(1, right, source.at[rows - EDGE : rows], target.at[:EDGE])
        send(-1, right, source.at[:EDGE], target.at[south_ms:north_pan])
        send(1, right, source.at[rows + depth - EDGE :], target.at[north_pan:south_pan])
        send(-1, right, source.at[rows : rows + EDGE], target.at[south_pan:])
    far_matrices = [ms_col_matrices(far_tap[end], far_frac[end]) for end in range(2)]
    wait_all(tall_steps, tall_copies)

    line = lax.broadcasted_iota(jnp.int32, (bands * EDGE, LANES), 0)
    lane = lax.broadcasted_iota(jnp.int32, (bands * EDGE, LANES), 1)
    chosen = (lane & (ms_slot - 1)) // MHALO == line // EDGE
    for end, lines in ((0, slice(0, EDGE)), (1, slice(EDGE + rows, 2 * EDGE + rows))):
        own_matrix, halo_matrix = far_matrices[end]
        side = jnp.concatenate([side_got[end]] * bands, axis=0)
        side = jnp.where(chosen, side.astype(jnp.float32), 0.0).astype(jnp.bfloat16)
        far = dot(seg_got[end].reshape(bands * EDGE, ms_cols), own_matrix) + dot(side, halo_matrix)
        for b in range(bands):
            wide[b + 1, lines, :] = far[b * EDGE : (b + 1) * EDGE].astype(jnp.bfloat16)
    clear(north_ok, wide.at[:, :EDGE, :])
    clear(south_ok, wide.at[:, EDGE + rows :, :])
    for got, ok in ((got_west, west_ok), (got_east, east_ok)):
        clear(ok, got)
        clear(north_ok, got.at[:EDGE])
        clear(south_ok, got.at[south_ms:north_pan])
        clear(north_ok, got.at[north_pan:south_pan])
        clear(south_ok, got.at[south_pan:])
    for got, shift, block in (
        (got_west, LANES - EDGE, slice(HALF - LANES, HALF)),
        (got_east, 0, slice(HALF, HALF + LANES)),
    ):
        line = lax.broadcasted_iota(jnp.int32, (LANES, GROUPS * LANES), 0)
        lane = lax.broadcasted_iota(jnp.int32, (LANES, GROUPS * LANES), 1)
        place_in = (lane & (LANES - 1)) - shift
        good = (place_in >= 0) & (place_in < EDGE) & (line == (lane // LANES) * EDGE + place_in)
        opener = jnp.where(good, 1.0, 0.0).astype(jnp.bfloat16)
        fields = dot(
            jnp.concatenate([got[: EDGE + rows], got[south_ms:north_pan]], axis=0), opener
        ).astype(jnp.bfloat16)
        for b in range(bands):
            wide[b + 1, :, block] += fields[:, b * LANES : (b + 1) * LANES]
        fields = dot(
            jnp.concatenate([got[EDGE + rows : south_ms], got[north_pan:]], axis=0), opener
        ).astype(jnp.bfloat16)
        for g in range(GROUPS):
            wide[0, EDGE + g * depth : EDGE + (g + 1) * depth, block] += fields[
                :depth, g * LANES : (g + 1) * LANES
            ]
        wide[0, :EDGE, block] += fields[depth : depth + EDGE, (GROUPS - 1) * LANES :]
        wide[0, EDGE + rows :, block] += fields[depth + EDGE :, :LANES]


def inv_cover(places, extent, ok):
    highest = jnp.minimum(places + RADIUS, extent - 1)
    lowest = jnp.maximum(places - RADIUS, 0)
    inside = (places >= 0) & (places < extent) & ok
    cover = jnp.where(inside, highest - lowest + 1, 1).astype(jnp.float32)
    return jnp.where(inside, 1.0 / cover, 0.0)

def sum_down(lines, pairs, fours, kept):
    count = kept + EDGE
    pairs[:count] = lines[:count] + lines[1 : count + 1]
    fours[:count] = pairs[:count] + pairs[2 : count + 2]
    eights = fours[: kept + 8] + fours[4 : kept + 12]
    return eights[:kept] + eights[8:] + lines[EDGE:count]


def setup(sec_count, tile_count, rows, cols, guide, cmat, amat, bmat, inverse, inverse_out, own):
    wide_rows = guide.shape[1]
    fit_rows = rows + EDGE
    placed, total = place(sec_count, tile_count)
    column = lax.rem(placed, GRID_COLS)
    grid_row = placed // GRID_COLS
    map_rows = total // GRID_COLS * rows
    map_cols = GRID_COLS * cols
    k = lax.broadcasted_iota(jnp.int32, (HALF, HALF), 0)
    j = lax.broadcasted_iota(jnp.int32, (HALF, HALF), 1)
    cmat[...] = jnp.where(((j - k + 2 * HALF) & (HALF - 1)) <= EDGE, 1.0, 0.0).astype(jnp.bfloat16)
    k = lax.broadcasted_iota(jnp.int32, (HALF, HALF), 0)
    j = lax.broadcasted_iota(jnp.int32, (HALF, HALF), 1)
    first_b = HALF - EDGE - EDGE
    amat[...] = jnp.where((k >= j) & (k - j <= EDGE) & (j < first_b), 1.0, 0.0).astype(jnp.bfloat16)
    off = cols - HALF
    fit_at = jnp.where(k < EDGE, HALF, 0) + k - RADIUS
    bmat[...] = jnp.where((jnp.abs(fit_at - j) <= RADIUS) & (j >= first_b - off) & ((k < EDGE) | (k >= 2 * EDGE)), 1.0, 0.0).astype(jnp.bfloat16)
    row0 = grid_row * rows
    col0 = column * cols
    lane = lax.broadcasted_iota(jnp.int32, (1, 2 * HALF), 1)
    in_b = lane >= HALF
    i = lane - HALF
    fit_col = jnp.where(in_b, jnp.where(i < EDGE, cols, off) + i - RADIUS, lane - RADIUS)
    ok = (lane < HALF - EDGE) | (in_b & ((i < EDGE) | (i >= 2 * EDGE)))
    line = lax.broadcasted_iota(jnp.int32, (fit_rows, 1), 0)
    inverse[...] = inv_cover(row0 - RADIUS + line, map_rows, line >= 0) * inv_cover(col0 + fit_col, map_cols, ok)
    line = lax.broadcasted_iota(jnp.int32, (rows, 1), 0)
    lane = lax.broadcasted_iota(jnp.int32, (1, cols), 1)
    inverse_out[...] = inv_cover(row0 + line, map_rows, line >= 0) * inv_cover(col0 + lane, map_cols, lane >= 0)
    mid = slice(EDGE, EDGE + rows)
    own[:, :LANES] = guide[0, mid, :LANES].astype(jnp.float32)
    l = lax.broadcasted_iota(jnp.int32, (rows, LANES), 1)
    own[:, LANES:2*LANES] = jnp.where(l < LANES // 2, guide[0, mid, LANES:2*LANES].astype(jnp.float32), guide[0, mid, HALF:HALF+LANES].astype(jnp.float32))
    own[:, 2*LANES:] = guide[0, mid, HALF + LANES:].astype(jnp.float32)

def split_dot(values, cmat):
    high = values.astype(jnp.bfloat16)
    low = (values - high.astype(jnp.float32)).astype(jnp.bfloat16)
    return dot(high, cmat[...]) + dot(low, cmat[...])

def put(target, values):
    for t in range(2):
        target[t, : values.shape[0]] = values[:, t * LANES : (t + 1) * LANES]

def filter_kernel(sec_count, tile_count, guide, bandref, out, cmat, amat, bmat, inverse, inverse_out, own, mean_guide, inverse_var, sums, fit, pairs, fours):
    rows, cols = out.shape[1:]
    fit_rows = rows + EDGE
    @pl.when(pl.program_id(0) == 0)
    def _():
        setup(sec_count, tile_count, rows, cols, guide, cmat, amat, bmat, inverse, inverse_out, own)
        for h in range(2):
            half = slice(h * HALF, (h + 1) * HALF)
            g = guide[0, :, half]
            gf = g.astype(jnp.float32)
            put(sums.at[h, 0], dot(g, cmat[...]))
            put(sums.at[h, 1], split_dot(gf * gf, cmat))
            for t in range(2):
                lanes = slice(h * HALF + t * LANES, h * HALF + (t + 1) * LANES)
                scale = inverse[:, lanes]
                mean = sum_down(sums.at[h, 0, t], pairs.at[h, 0, t], fours.at[h, 0, t], fit_rows) * scale
                square = sum_down(sums.at[h, 1, t], pairs.at[h, 1, t], fours.at[h, 1, t], fit_rows) * scale
                mean_guide[:, lanes] = mean
                inverse_var[:, lanes] = 1.0 / (square - mean * mean + EPSILON)
    for h in range(2):
        half = slice(h * HALF, (h + 1) * HALF)
        p = bandref[0, :, half]
        put(sums.at[h, 0], dot(p, cmat[...]))
        put(sums.at[h, 1], split_dot(guide[0, :, half].astype(jnp.float32) * p.astype(jnp.float32), cmat))
    for h in range(2):
        for t in range(2):
            lanes = slice(h * HALF + t * LANES, h * HALF + (t + 1) * LANES)
            scale = inverse[:, lanes]
            mean = mean_guide[:, lanes]
            mean_band = sum_down(sums.at[h, 0, t], pairs.at[h, 0, t], fours.at[h, 0, t], fit_rows) * scale
            cross = sum_down(sums.at[h, 1, t], pairs.at[h, 1, t], fours.at[h, 1, t], fit_rows) * scale
            gain = (cross - mean * mean_band) * inverse_var[:, lanes]
            fit[h, 0, :, t * LANES : (t + 1) * LANES] = gain.astype(jnp.bfloat16)
            fit[h, 1, :, t * LANES : (t + 1) * LANES] = (mean_band - gain * mean).astype(jnp.bfloat16)
    for q in range(2):
        a = dot(fit[0, q], amat[...])
        b = dot(fit[1, q], bmat[...])
        sums[0, q, 0, :fit_rows] = a[:, :LANES]
        sums[0, q, 1, :fit_rows] = a[:, LANES:] + b[:, :LANES]
        sums[1, q, 0, :fit_rows] = b[:, LANES:]
    for t in range(3):
        lanes = slice(t * LANES, (t + 1) * LANES)
        gain = sum_down(sums.at[t // 2, 0, t % 2], pairs.at[t // 2, 0, t % 2], fours.at[t // 2, 0, t % 2], rows)
        offset = sum_down(sums.at[t // 2, 1, t % 2], pairs.at[t // 2, 1, t % 2], fours.at[t // 2, 1, t % 2], rows)
        out[0, :, lanes] = ((gain * own[:, lanes] + offset) * inverse_out[:, lanes]).astype(jnp.bfloat16)

def local(sec_count, tile_count, pan_source, ms_source, *tables):
    rows, cols = pan_source.shape[1:]
    bands, _, ms_rows, ms_cols = ms_source.shape
    channels = bands + 1
    wide_rows = rows + 2 * EDGE
    width = 2 * HALF
    dense_rows = rows + rows // GROUPS
    bf16, f32 = jnp.bfloat16, jnp.float32
    vmem = pl.BlockSpec(memory_space=pltpu.VMEM)
    dma = pltpu.SemaphoreType.DMA
    wide = pl.pallas_call(
        functools.partial(resample_kernel, sec_count, tile_count),
        out_shape=jax.ShapeDtypeStruct((channels, wide_rows, width), bf16),
        in_specs=[pl.BlockSpec(memory_space=pltpu.HBM)] * (2 + len(tables)),
        out_specs=vmem,
        scratch_shapes=[pltpu.VMEM((bands, ms_rows, ms_cols), bf16)]
        + [pltpu.VMEM(table.shape, table.dtype) for table in tables]
        + [
            pltpu.VMEM((2,) + tables[6].shape, tables[6].dtype),
            pltpu.VMEM((2,) + tables[7].shape, tables[7].dtype),
            pltpu.VMEM((2, bands, EDGE, ms_cols), bf16),
            pltpu.VMEM((2, bands, EDGE, ms_cols), bf16),
            pltpu.VMEM((2, EDGE, LANES), bf16),
            pltpu.VMEM((2, EDGE, LANES), bf16),
            pltpu.VMEM((rows + 2 * HALO, cols + 2 * LANES), bf16),
            pltpu.VMEM((2, bands // 2, 16, ms_cols), bf16),
            pltpu.VMEM((2, bands // 2, 16, ms_cols), bf16),
            pltpu.VMEM((2, rows * HALO // LANES, LANES), bf16),
            pltpu.VMEM((2, rows * HALO // LANES, LANES), bf16),
            pltpu.VMEM((2, ms_rows, LANES), bf16),
            pltpu.VMEM((2, ms_rows + 32, LANES), bf16),
            pltpu.VMEM((dense_rows, LANES), bf16),
            pltpu.VMEM((dense_rows, LANES), bf16),
            pltpu.VMEM((dense_rows + 4 * EDGE, LANES), bf16),
            pltpu.VMEM((dense_rows + 4 * EDGE, LANES), bf16),
            dma,
            dma((len(tables) + 1,)),
        ]
        + [dma((len(STEPS),))] * 4
        + [dma((18,))] * 2
        + [dma((4,))] * 2,
        compiler_params=pltpu.CompilerParams(collective_id=0, has_side_effects=True),
    )(pan_source.reshape(rows, cols), ms_source.reshape(bands, ms_rows, ms_cols), *tables)
    fit_rows = rows + EDGE
    sharpened = pl.pallas_call(
        functools.partial(filter_kernel, sec_count, tile_count),
        grid=(bands,),
        out_shape=jax.ShapeDtypeStruct((bands, rows, cols), bf16),
        in_specs=[
            pl.BlockSpec((1, wide_rows, width), lambda b: (0, 0, 0)),
            pl.BlockSpec((1, wide_rows, width), lambda b: (b + 1, 0, 0)),
        ],
        out_specs=pl.BlockSpec((1, rows, cols), lambda b: (b, 0, 0)),
        scratch_shapes=[
            pltpu.VMEM((HALF, HALF), bf16),
            pltpu.VMEM((HALF, HALF), bf16),
            pltpu.VMEM((HALF, HALF), bf16),
            pltpu.VMEM((fit_rows, width), f32),
            pltpu.VMEM((rows, cols), f32),
            pltpu.VMEM((rows, cols), f32),
            pltpu.VMEM((fit_rows, width), f32),
            pltpu.VMEM((fit_rows, width), f32),
            pltpu.VMEM((2, 2, 2, wide_rows + EDGE, LANES), f32),
            pltpu.VMEM((2, 2, fit_rows, HALF), bf16),
            pltpu.VMEM((2, 2, 2, wide_rows + EDGE, LANES), f32),
            pltpu.VMEM((2, 2, 2, wide_rows + EDGE, LANES), f32),
        ],
    )(wide, wide)
    return sharpened[:, None]


def solution(mesh):
    tiles = ("sec", "tile")
    table = P(tiles, None)
    return jax.shard_map(
        functools.partial(local, mesh.shape["sec"], mesh.shape["tile"]),
        mesh=mesh,
        in_specs=(P(tiles, None, None), P(None, tiles, None, None)) + (table,) * 8,
        out_specs=P(None, tiles, None, None),
        check_vma=False,
    )
```

```python
import functools

import jax
import jax.numpy as jnp
from jax import lax
from jax.experimental import pallas as pl
from jax.experimental.pallas import tpu as pltpu
from jax.sharding import PartitionSpec as P

HALO = 32
MHALO = 8
RADIUS = 8
EPSILON = 0.1
GRID_COLS = 4
EDGE = 2 * RADIUS
LANES = 128
HALF = 256
GROUPS = 8
NOWHERE = -1000
MESH = pl.DeviceIdType.MESH

STEPS = ((1, 0), (-1, 0), (0, 1), (0, -1), (1, 1), (1, -1), (-1, 1), (-1, -1))


def cubic_weights(fraction):
    squared = fraction * fraction
    cubed = squared * fraction
    return (
        -0.5 * cubed + squared - 0.5 * fraction,
        1.5 * cubed - 2.5 * squared + 1.0,
        -1.5 * cubed + 2.0 * squared + 0.5 * fraction,
        0.5 * cubed - 0.5 * squared,
    )


def band(taps, fraction, length, shift):
    line = lax.broadcasted_iota(jnp.int32, (length, taps.shape[1]), 0)
    return band_at(line - shift, taps, fraction)


def band_at(position, taps, fraction):
    weights = cubic_weights(fraction)
    distance = position - taps
    matrix = jnp.zeros(position.shape, jnp.float32)
    for offset in range(4):
        matrix = jnp.where(distance == offset, weights[offset], matrix)
    return matrix.astype(jnp.bfloat16)


def spread(values, fill):
    lane = lax.broadcasted_iota(jnp.int32, (1, 2 * HALF), 1)
    both = jnp.concatenate([values[:, :HALF], values[:, values.shape[1] - HALF :]], axis=1)
    return jnp.where((lane >= HALF - EDGE) & (lane < HALF + EDGE), fill, both).astype(values.dtype)


def picker(shape, shift, low, high):
    source = lax.broadcasted_iota(jnp.int32, shape, 0)
    target = lax.broadcasted_iota(jnp.int32, shape, 1)
    chosen = (target - source == shift) & (source >= low) & (source < high)
    return jnp.where(chosen, 1.0, 0.0).astype(jnp.bfloat16)


def dot(left, right):
    return jnp.dot(left, right, preferred_element_type=jnp.float32)


def dot_t(left, right):
    return lax.dot_general(
        left, right, (((0,), (0,)), ((), ())), preferred_element_type=jnp.float32
    )


def place(sec_count, tile_count):
    total = sec_count * tile_count
    me = lax.axis_index("sec") * tile_count + lax.axis_index("tile")
    return lax.rem(me + 2, total), total


def resample_kernel(
    sec_count,
    tile_count,
    pan,
    ms,
    row_tap,
    row_frac,
    col_tap,
    col_frac,
    ms_row_tap,
    ms_row_frac,
    ms_col_tap,
    ms_col_frac,
    out,
    wide,
    ms_own,
    row_tap_here,
    row_frac_here,
    col_tap_here,
    col_frac_here,
    ms_row_tap_here,
    ms_row_frac_here,
    ms_col_tap_here,
    ms_col_frac_here,
    far_tap,
    far_frac,
    seg_edge,
    seg_got,
    side_edge,
    side_got,
    pan_patch,
    ms_vert,
    ms_tall,
    pan_pack,
    pan_got,
    ms_pack,
    ms_got,
    packs_pan,
    packs_ms,
    gots_pan,
    gots_ms,
    cmat,
    amat,
    bmat,
    inverse,
    inverse_out,
    own_guide,
    mean_guide,
    inverse_var,
    sums,
    fit,
    pairs,
    fours,
    local_sem,
    table_sem,
    send_pan,
    recv_pan,
    send_ms,
    recv_ms,
    send_tall,
    recv_tall,
    send_table,
    recv_table,
):
    rows, cols = pan.shape
    bands, ms_rows, ms_cols = ms.shape
    placed, total = place(sec_count, tile_count)
    column = lax.rem(placed, GRID_COLS)
    grid_row = placed // GRID_COLS
    north_ok = grid_row > 0
    south_ok = grid_row < total // GRID_COLS - 1
    west_ok = column > 0
    east_ok = column < GRID_COLS - 1

    def device(down, right):
        there = lax.rem(placed + down * GRID_COLS + right - 2 + 2 * total, total)
        return (there // tile_count, lax.rem(there, tile_count))

    def reaches(down, right):
        ok = True
        if down:
            ok = south_ok if down > 0 else north_ok
        if right:
            side = east_ok if right > 0 else west_ok
            ok = side if ok is True else ok & side
        return ok

    def start_all(steps, copies):
        for (down, right), copy in zip(steps, copies):
            pl.when(reaches(down, right))(copy.start)

    def wait_all(steps, copies):
        for (down, right), copy in zip(steps, copies):
            pl.when(reaches(-down, -right))(copy.wait_recv)
        for (down, right), copy in zip(steps, copies):
            pl.when(reaches(down, right))(copy.wait_send)

    barrier = pltpu.get_barrier_semaphore()
    for down, right in STEPS:

        @pl.when(reaches(down, right))
        def _(down=down, right=right):
            pl.semaphore_signal(
                barrier, inc=1, device_id=device(down, right), device_id_type=MESH
            )

    own_copy = pltpu.make_async_copy(
        pan, pan_patch.at[HALO : HALO + rows, LANES : LANES + cols], local_sem
    )
    fetched = [
        pltpu.make_async_copy(source, target, table_sem.at[index])
        for index, (source, target) in enumerate(
            (
                (row_tap, row_tap_here),
                (row_frac, row_frac_here),
                (col_tap, col_tap_here),
                (col_frac, col_frac_here),
                (ms_row_tap, ms_row_tap_here),
                (ms_row_frac, ms_row_frac_here),
                (ms_col_tap, ms_col_tap_here),
                (ms_col_frac, ms_col_frac_here),
                (ms, ms_own),
            )
        )
    ]
    for copy in fetched:
        copy.start()
    own_copy.start()
    for copy in fetched:
        copy.wait()
    own_copy.wait()
    group = rows // (LANES // HALO)
    ms_slot = LANES // 2
    for side in range(2):
        total_pan = jnp.zeros((group, LANES), jnp.float32)
        first_lane = 0 if side else LANES - HALO
        block = slice(LANES, 2 * LANES) if side else slice(cols, cols + LANES)
        for g in range(LANES // HALO):
            move = picker(
                (LANES, LANES), g * HALO - first_lane, first_lane, first_lane + HALO
            )
            lines = slice(HALO + g * group, HALO + (g + 1) * group)
            total_pan = total_pan + dot(pan_patch[lines, block], move)
        pan_pack[side] = total_pan.astype(jnp.bfloat16)
        total_ms = jnp.zeros((ms_rows, LANES), jnp.float32)
        first_lane = 0 if side else ms_cols - MHALO
        for b in range(bands):
            move = picker(
                (ms_cols, LANES),
                side * ms_slot + b * MHALO - first_lane,
                first_lane,
                first_lane + MHALO,
            )
            total_ms = total_ms + dot(ms_own[b], move)
        ms_pack[side] = total_ms.astype(jnp.bfloat16)
        lines = slice(0, MHALO) if side else slice(ms_rows - MHALO, ms_rows)
        for pair in range(bands // 2):
            both = [ms_own[b].astype(jnp.float32)[lines] for b in (2 * pair, 2 * pair + 1)]
            ms_tall[side, pair] = jnp.concatenate(both, axis=0).astype(jnp.bfloat16)

    tall = 1 + north_ok.astype(jnp.int32) + south_ok.astype(jnp.int32)
    broad = 1 + west_ok.astype(jnp.int32) + east_ok.astype(jnp.int32)
    pl.semaphore_wait(barrier, tall * broad - 1)

    def span(step, size, depth):
        if step > 0:
            return slice(size - depth, size), slice(0, depth)
        if step < 0:
            return slice(0, depth), slice(depth + size, 2 * depth + size)
        return slice(0, size), slice(depth, depth + size)

    steps, copies = [], []
    for index, (down, right) in enumerate(STEPS):
        row_from, row_to = span(down, rows, HALO)
        col_from, col_to = span(right, cols, LANES)
        side = 0 if right > 0 else 1
        if down:
            source, target = pan.at[row_from, col_from], pan_patch.at[row_to, col_to]
        else:
            source, target = pan_pack.at[side], pan_got.at[side]
        steps.append((down, right))
        copies.append(
            pltpu.make_async_remote_copy(
                src_ref=source,
                dst_ref=target,
                send_sem=send_pan.at[index],
                recv_sem=recv_pan.at[index],
                device_id=device(down, right),
                device_id_type=MESH,
            )
        )
        row_from, row_to = span(down, ms_rows, 16)
        if right:
            source, target = ms_pack.at[side, row_from, :], ms_got.at[side, row_to, :]
        else:
            source, target = ms_tall.at[0 if down > 0 else 1], ms_vert.at[0 if down > 0 else 1]
        steps.append((down, right))
        copies.append(
            pltpu.make_async_remote_copy(
                src_ref=source,
                dst_ref=target,
                send_sem=send_ms.at[index],
                recv_sem=recv_ms.at[index],
                device_id=device(down, right),
                device_id_type=MESH,
            )
        )
    for index, down in enumerate((1, -1)):
        for which, (source, target) in enumerate(((ms_col_tap, far_tap), (ms_col_frac, far_frac))):
            steps.append((down, 0))
            copies.append(
                pltpu.make_async_remote_copy(
                    src_ref=source,
                    dst_ref=target.at[index],
                    send_sem=send_table.at[2 * index + which],
                    recv_sem=recv_table.at[2 * index + which],
                    device_id=device(down, 0),
                    device_id_type=MESH,
                )
            )
    start_all(steps, copies)
    row_matrix = band(row_tap_here[...], row_frac_here[...], 2 * HALO + rows, 0)
    col_matrix = band(
        spread(col_tap_here[...], NOWHERE), spread(col_frac_here[...], 0), 2 * LANES + cols, LANES - HALO
    )
    ms_row_taps = ms_row_tap_here[...]
    ms_row_fracs = ms_row_frac_here[...]
    ms_row_matrix = band(ms_row_taps, ms_row_fracs, 32 + ms_rows, 16 - MHALO)
    line = lax.broadcasted_iota(jnp.int32, (32 + ms_rows, rows), 0)
    below = 16 + ms_rows
    away = -LANES
    first_of_pair = jnp.where(
        line < MHALO, line, jnp.where((line < 16) | (line >= below + MHALO), away, line - MHALO)
    )
    second_of_pair = jnp.where(
        line < MHALO,
        away,
        jnp.where(
            line < below, line - MHALO, jnp.where(line < below + MHALO, away, line - 2 * MHALO)
        ),
    )
    ms_pair_matrices = tuple(
        band_at(position, ms_row_taps, ms_row_fracs)
        for position in (first_of_pair, second_of_pair)
    )

    def ms_col_matrices(taps, fracs):
        taps, fracs = spread(taps, NOWHERE), spread(fracs, 0)
        lane = lax.broadcasted_iota(jnp.int32, (LANES, taps.shape[1]), 0)
        position = jnp.where(lane < ms_slot, 0, ms_cols + MHALO) + (lane & (MHALO - 1))
        return band(taps, fracs, ms_cols, -MHALO), band_at(position, taps, fracs)

    ms_own_matrix, ms_halo_matrix = ms_col_matrices(ms_col_tap_here[...], ms_col_frac_here[...])
    packers = []
    for shift in (LANES - EDGE, 0):
        line = lax.broadcasted_iota(jnp.int32, (GROUPS * LANES, LANES), 0)
        lane = lax.broadcasted_iota(jnp.int32, (GROUPS * LANES, LANES), 1)
        place_in = (line & (LANES - 1)) - shift
        good = (place_in >= 0) & (place_in < EDGE) & (lane == (line // LANES) * EDGE + place_in)
        packers.append(jnp.where(good, 1.0, 0.0).astype(jnp.bfloat16))

    wait_all(steps, copies)

    def clear(ok, ref):
        @pl.when(jnp.logical_not(ok))
        def _():
            ref[...] = jnp.zeros(ref.shape, ref.dtype)

    clear(west_ok, pan_got.at[0])
    clear(east_ok, pan_got.at[1])
    for side in range(2):
        first_lane = 0 if side else LANES - HALO
        block = slice(LANES + cols, 2 * LANES + cols) if side else slice(0, LANES)
        for g in range(LANES // HALO):
            move = picker((LANES, LANES), first_lane - g * HALO, g * HALO, (g + 1) * HALO)
            lines = slice(HALO + g * group, HALO + (g + 1) * group)
            pan_patch[lines, block] = dot(pan_got[side], move).astype(jnp.bfloat16)

    clear(north_ok, pan_patch.at[:HALO, :])
    clear(south_ok, pan_patch.at[HALO + rows :, :])
    clear(west_ok, pan_patch.at[:, :LANES])
    clear(east_ok, pan_patch.at[:, LANES + cols :])
    clear(north_ok, ms_vert.at[0])
    clear(south_ok, ms_vert.at[1])
    for side, ok in ((0, west_ok), (1, east_ok)):
        clear(ok, ms_got.at[side])
        clear(north_ok, ms_got.at[side, :16, :])
        clear(south_ok, ms_got.at[side, 16 + ms_rows :, :])

    groups = []

    def send(down, right, source, target):
        index = sum(len(group) for group in groups)
        copy = pltpu.make_async_remote_copy(
            src_ref=source,
            dst_ref=target,
            send_sem=send_tall.at[index],
            recv_sem=recv_tall.at[index],
            device_id=device(down, right),
            device_id_type=MESH,
        )
        groups[-1].append(((down, right), copy))
        start_all([(down, right)], [copy])

    mid = slice(EDGE, EDGE + rows)
    ends = (slice(rows - EDGE, rows), slice(0, EDGE))
    edge_blocks = (slice(2 * HALF - LANES, 2 * HALF), slice(0, LANES))

    def send_sides(channels, packs, gots):
        folds = GROUPS // len(channels)
        depth = rows // folds
        for side, right in ((0, 1), (1, -1)):
            fields = [
                wide[c, EDGE + f * depth : EDGE + (f + 1) * depth, edge_blocks[side]]
                for f in range(folds)
                for c in channels
            ]
            pack, got = packs.at[side], gots.at[side]
            pack[...] = dot(jnp.concatenate(fields, axis=1), packers[side]).astype(jnp.bfloat16)
            send(0, right, pack, got.at[:depth])
            send(1, right, pack.at[depth - EDGE :], got.at[depth : depth + EDGE])
            send(-1, right, pack.at[:EDGE], got.at[depth + EDGE :])

    def open_sides(channels, gots):
        folds = GROUPS // len(channels)
        depth = rows // folds
        count = len(channels)
        for side, ok, block in (
            (0, west_ok, slice(HALF - LANES, HALF)),
            (1, east_ok, slice(HALF, HALF + LANES)),
        ):
            got = gots.at[side]
            clear(ok, got)
            clear(north_ok, got.at[depth : depth + EDGE])
            clear(south_ok, got.at[depth + EDGE :])
            fields = dot(got[...], openers[side]).astype(jnp.bfloat16)
            for index, c in enumerate(channels):
                part = lambda f: fields[:, (f * count + index) * LANES : (f * count + index + 1) * LANES]
                for f in range(folds):
                    wide[c, EDGE + f * depth : EDGE + (f + 1) * depth, block] += part(f)[:depth]
                wide[c, :EDGE, block] += part(folds - 1)[depth : depth + EDGE]
                wide[c, EDGE + rows :, block] += part(0)[depth + EDGE :]

    def wait_group(group):
        wait_all([step for step, _ in group], [copy for _, copy in group])

    groups.append([])
    segment = dot_t(row_matrix, pan_patch[...]).astype(jnp.bfloat16)
    wide[0, mid, :] = dot(segment, col_matrix).astype(jnp.bfloat16)
    send(1, 0, wide.at[0, rows : rows + EDGE], wide.at[0, :EDGE])
    send(-1, 0, wide.at[0, EDGE : 2 * EDGE], wide.at[0, EDGE + rows :])
    send_sides((0,), packs_pan, gots_pan)
    lane = lax.broadcasted_iota(jnp.int32, (rows, LANES), 1)
    halo_segment = dot_t(ms_row_matrix, ms_got[0]) + dot_t(ms_row_matrix, ms_got[1])
    halo_band = (lane & (ms_slot - 1)) // MHALO
    per_group = bands // 2
    for group in range(2):
        groups.append([])
        if group == 0:
            for end in range(2):
                side_edge[end] = halo_segment[ends[end]].astype(jnp.bfloat16)
                send(1 - 2 * end, 0, side_edge.at[end], side_got.at[end])
        members = range(group * per_group, (group + 1) * per_group)
        for b in members:
            block = jnp.concatenate([ms_vert[0, b // 2], ms_own[b], ms_vert[1, b // 2]], axis=0)
            segment = dot_t(ms_pair_matrices[b % 2], block).astype(jnp.bfloat16)
            for end in range(2):
                seg_edge[end, b] = segment[ends[end]]
            beside = jnp.where(halo_band == b, halo_segment, 0.0).astype(jnp.bfloat16)
            wide[b + 1, mid, :] = (
                dot(segment, ms_own_matrix) + dot(beside, ms_halo_matrix)
            ).astype(jnp.bfloat16)
        for end in range(2):
            part = slice(group * per_group, (group + 1) * per_group)
            send(1 - 2 * end, 0, seg_edge.at[end, part], seg_got.at[end, part])
        send_sides(tuple(b + 1 for b in members), packs_ms.at[group], gots_ms.at[group])

    setup(placed, total, rows, cols, wide, cmat, amat, bmat, inverse, inverse_out, own_guide)
    openers = []
    for shift in (LANES - EDGE, 0):
        line = lax.broadcasted_iota(jnp.int32, (LANES, GROUPS * LANES), 0)
        lane = lax.broadcasted_iota(jnp.int32, (LANES, GROUPS * LANES), 1)
        place_in = (lane & (LANES - 1)) - shift
        good = (place_in >= 0) & (place_in < EDGE) & (line == (lane // LANES) * EDGE + place_in)
        openers.append(jnp.where(good, 1.0, 0.0).astype(jnp.bfloat16))
    far_matrices = [ms_col_matrices(far_tap[end], far_frac[end]) for end in range(2)]

    wait_group(groups[0])
    clear(north_ok, wide.at[0, :EDGE])
    clear(south_ok, wide.at[0, EDGE + rows :])
    open_sides((0,), gots_pan)
    guide_stats(rows, wide, cmat, inverse, mean_guide, inverse_var, sums, pairs, fours)
    line = lax.broadcasted_iota(jnp.int32, (per_group * EDGE, LANES), 0)
    lane = lax.broadcasted_iota(jnp.int32, (per_group * EDGE, LANES), 1)
    for group in range(2):
        first = group * per_group
        wait_group(groups[group + 1])
        chosen = (lane & (ms_slot - 1)) // MHALO == line // EDGE + first
        for end, lines in ((0, slice(0, EDGE)), (1, slice(EDGE + rows, 2 * EDGE + rows))):
            own_matrix, halo_matrix = far_matrices[end]
            side = jnp.concatenate([side_got[end]] * per_group, axis=0)
            side = jnp.where(chosen, side.astype(jnp.float32), 0.0).astype(jnp.bfloat16)
            piece = seg_got[end, first : first + per_group].reshape(per_group * EDGE, ms_cols)
            far = dot(piece, own_matrix) + dot(side, halo_matrix)
            for b in range(per_group):
                wide[first + b + 1, lines, :] = far[b * EDGE : (b + 1) * EDGE].astype(jnp.bfloat16)
        members = slice(first + 1, first + per_group + 1)
        clear(north_ok, wide.at[members, :EDGE, :])
        clear(south_ok, wide.at[members, EDGE + rows :, :])
        open_sides(tuple(range(first + 1, first + per_group + 1)), gots_ms.at[group])

        def one_band(b, carry):
            filter_band(
                rows,
                wide.at[0],
                wide.at[b + 1],
                out.at[b],
                cmat,
                amat,
                bmat,
                inverse,
                inverse_out,
                own_guide,
                mean_guide,
                inverse_var,
                sums,
                fit,
                pairs,
                fours,
            )
            return carry

        lax.fori_loop(first, first + per_group, one_band, 0)


def sum_down(lines, pairs, fours, kept):
    count = kept + EDGE
    pairs[:count] = lines[:count] + lines[1 : count + 1]
    fours[:count] = pairs[:count] + pairs[2 : count + 2]
    eights = fours[: kept + 8] + fours[4 : kept + 12]
    return eights[:kept] + eights[8:] + lines[EDGE:count]


def inv_cover(places, extent, ok):
    highest = jnp.minimum(places + RADIUS, extent - 1)
    lowest = jnp.maximum(places - RADIUS, 0)
    inside = (places >= 0) & (places < extent) & ok
    cover = jnp.where(inside, highest - lowest + 1, 1).astype(jnp.float32)
    return jnp.where(inside, 1.0 / cover, 0.0)

def sum_down(lines, pairs, fours, kept):
    count = kept + EDGE
    pairs[:count] = lines[:count] + lines[1 : count + 1]
    fours[:count] = pairs[:count] + pairs[2 : count + 2]
    eights = fours[: kept + 8] + fours[4 : kept + 12]
    return eights[:kept] + eights[8:] + lines[EDGE:count]


def setup(placed, total, rows, cols, guide, cmat, amat, bmat, inverse, inverse_out, own):
    fit_rows = rows + EDGE
    column = lax.rem(placed, GRID_COLS)
    grid_row = placed // GRID_COLS
    map_rows = total // GRID_COLS * rows
    map_cols = GRID_COLS * cols
    k = lax.broadcasted_iota(jnp.int32, (HALF, HALF), 0)
    j = lax.broadcasted_iota(jnp.int32, (HALF, HALF), 1)
    cmat[...] = jnp.where(((j - k + 2 * HALF) & (HALF - 1)) <= EDGE, 1.0, 0.0).astype(jnp.bfloat16)
    k = lax.broadcasted_iota(jnp.int32, (HALF, HALF), 0)
    j = lax.broadcasted_iota(jnp.int32, (HALF, HALF), 1)
    first_b = HALF - EDGE - EDGE
    amat[...] = jnp.where((k >= j) & (k - j <= EDGE) & (j < first_b), 1.0, 0.0).astype(jnp.bfloat16)
    off = cols - HALF
    fit_at = jnp.where(k < EDGE, HALF, 0) + k - RADIUS
    bmat[...] = jnp.where((jnp.abs(fit_at - j) <= RADIUS) & (j >= first_b - off) & ((k < EDGE) | (k >= 2 * EDGE)), 1.0, 0.0).astype(jnp.bfloat16)
    row0 = grid_row * rows
    col0 = column * cols
    lane = lax.broadcasted_iota(jnp.int32, (1, 2 * HALF), 1)
    in_b = lane >= HALF
    i = lane - HALF
    fit_col = jnp.where(in_b, jnp.where(i < EDGE, cols, off) + i - RADIUS, lane - RADIUS)
    ok = (lane < HALF - EDGE) | (in_b & ((i < EDGE) | (i >= 2 * EDGE)))
    line = lax.broadcasted_iota(jnp.int32, (fit_rows, 1), 0)
    inverse[...] = inv_cover(row0 - RADIUS + line, map_rows, line >= 0) * inv_cover(col0 + fit_col, map_cols, ok)
    line = lax.broadcasted_iota(jnp.int32, (rows, 1), 0)
    lane = lax.broadcasted_iota(jnp.int32, (1, cols), 1)
    inverse_out[...] = inv_cover(row0 + line, map_rows, line >= 0) * inv_cover(col0 + lane, map_cols, lane >= 0)
    mid = slice(EDGE, EDGE + rows)
    own[:, :LANES] = guide[0, mid, :LANES].astype(jnp.float32)
    l = lax.broadcasted_iota(jnp.int32, (rows, LANES), 1)
    own[:, LANES:2*LANES] = jnp.where(l < LANES // 2, guide[0, mid, LANES:2*LANES].astype(jnp.float32), guide[0, mid, HALF:HALF+LANES].astype(jnp.float32))
    own[:, 2*LANES:] = guide[0, mid, HALF + LANES:].astype(jnp.float32)

def split_dot(values, cmat):
    high = values.astype(jnp.bfloat16)
    low = (values - high.astype(jnp.float32)).astype(jnp.bfloat16)
    return dot(high, cmat[...]) + dot(low, cmat[...])

def put(target, values):
    for t in range(2):
        target[t, : values.shape[0]] = values[:, t * LANES : (t + 1) * LANES]

def guide_stats(rows, guide, cmat, inverse, mean_guide, inverse_var, sums, pairs, fours):
    fit_rows = rows + EDGE
    for h in range(2):
        half = slice(h * HALF, (h + 1) * HALF)
        g = guide[0, :, half]
        gf = g.astype(jnp.float32)
        put(sums.at[h, 0], dot(g, cmat[...]))
        put(sums.at[h, 1], split_dot(gf * gf, cmat))
        for t in range(2):
            lanes = slice(h * HALF + t * LANES, h * HALF + (t + 1) * LANES)
            scale = inverse[:, lanes]
            mean = sum_down(sums.at[h, 0, t], pairs.at[h, 0, t], fours.at[h, 0, t], fit_rows) * scale
            square = sum_down(sums.at[h, 1, t], pairs.at[h, 1, t], fours.at[h, 1, t], fit_rows) * scale
            mean_guide[:, lanes] = mean
            inverse_var[:, lanes] = 1.0 / (square - mean * mean + EPSILON)


def filter_band(
    rows,
    guide,
    bandref,
    out,
    cmat,
    amat,
    bmat,
    inverse,
    inverse_out,
    own,
    mean_guide,
    inverse_var,
    sums,
    fit,
    pairs,
    fours,
):
    fit_rows = rows + EDGE
    for h in range(2):
        half = slice(h * HALF, (h + 1) * HALF)
        p = bandref[:, half]
        put(sums.at[h, 0], dot(p, cmat[...]))
        put(sums.at[h, 1], split_dot(guide[:, half].astype(jnp.float32) * p.astype(jnp.float32), cmat))
    for h in range(2):
        for t in range(2):
            lanes = slice(h * HALF + t * LANES, h * HALF + (t + 1) * LANES)
            scale = inverse[:, lanes]
            mean = mean_guide[:, lanes]
            mean_band = sum_down(sums.at[h, 0, t], pairs.at[h, 0, t], fours.at[h, 0, t], fit_rows) * scale
            cross = sum_down(sums.at[h, 1, t], pairs.at[h, 1, t], fours.at[h, 1, t], fit_rows) * scale
            gain = (cross - mean * mean_band) * inverse_var[:, lanes]
            fit[h, 0, :, t * LANES : (t + 1) * LANES] = gain.astype(jnp.bfloat16)
            fit[h, 1, :, t * LANES : (t + 1) * LANES] = (mean_band - gain * mean).astype(jnp.bfloat16)
    for q in range(2):
        a = dot(fit[0, q], amat[...])
        b = dot(fit[1, q], bmat[...])
        sums[0, q, 0, :fit_rows] = a[:, :LANES]
        sums[0, q, 1, :fit_rows] = a[:, LANES:] + b[:, :LANES]
        sums[1, q, 0, :fit_rows] = b[:, LANES:]
    for t in range(3):
        lanes = slice(t * LANES, (t + 1) * LANES)
        gain = sum_down(sums.at[t // 2, 0, t % 2], pairs.at[t // 2, 0, t % 2], fours.at[t // 2, 0, t % 2], rows)
        offset = sum_down(sums.at[t // 2, 1, t % 2], pairs.at[t // 2, 1, t % 2], fours.at[t // 2, 1, t % 2], rows)
        out[:, lanes] = ((gain * own[:, lanes] + offset) * inverse_out[:, lanes]).astype(jnp.bfloat16)

def local(sec_count, tile_count, pan_source, ms_source, *tables):
    rows, cols = pan_source.shape[1:]
    bands, _, ms_rows, ms_cols = ms_source.shape
    channels = bands + 1
    wide_rows = rows + 2 * EDGE
    width = 2 * HALF
    dense_rows = rows + rows // GROUPS
    fit_rows = rows + EDGE
    depth = rows // GROUPS
    half_bands = bands // 2
    fold_rows = rows * half_bands // GROUPS
    bf16, f32 = jnp.bfloat16, jnp.float32
    dma = pltpu.SemaphoreType.DMA
    hbm = pl.BlockSpec(memory_space=pltpu.HBM)
    operands = (pan_source.reshape(rows, cols), ms_source.reshape(bands, ms_rows, ms_cols)) + tables
    sharpened = pl.pallas_call(
        functools.partial(resample_kernel, sec_count, tile_count),
        out_shape=pltpu.VMEM((bands, rows, cols), bf16),
        in_specs=[hbm] * (2 + len(tables)),
        out_specs=pl.BlockSpec(memory_space=pltpu.VMEM),
        scratch_shapes=[
            pltpu.VMEM((channels, wide_rows, width), bf16),
            pltpu.VMEM((bands, ms_rows, ms_cols), bf16),
        ]
        + [pltpu.VMEM(table.shape, table.dtype) for table in tables]
        + [
            pltpu.VMEM((2,) + tables[6].shape, tables[6].dtype),
            pltpu.VMEM((2,) + tables[7].shape, tables[7].dtype),
            pltpu.VMEM((2, bands, EDGE, ms_cols), bf16),
            pltpu.VMEM((2, bands, EDGE, ms_cols), bf16),
            pltpu.VMEM((2, EDGE, LANES), bf16),
            pltpu.VMEM((2, EDGE, LANES), bf16),
            pltpu.VMEM((rows + 2 * HALO, cols + 2 * LANES), bf16),
            pltpu.VMEM((2, bands // 2, 16, ms_cols), bf16),
            pltpu.VMEM((2, bands // 2, 16, ms_cols), bf16),
            pltpu.VMEM((2, rows * HALO // LANES, LANES), bf16),
            pltpu.VMEM((2, rows * HALO // LANES, LANES), bf16),
            pltpu.VMEM((2, ms_rows, LANES), bf16),
            pltpu.VMEM((2, ms_rows + 32, LANES), bf16),
            pltpu.VMEM((2, depth, LANES), bf16),
            pltpu.VMEM((2, 2, fold_rows, LANES), bf16),
            pltpu.VMEM((2, depth + 2 * EDGE, LANES), bf16),
            pltpu.VMEM((2, 2, fold_rows + 2 * EDGE, LANES), bf16),
            pltpu.VMEM((HALF, HALF), bf16),
            pltpu.VMEM((HALF, HALF), bf16),
            pltpu.VMEM((HALF, HALF), bf16),
            pltpu.VMEM((fit_rows, width), f32),
            pltpu.VMEM((rows, cols), f32),
            pltpu.VMEM((rows, cols), f32),
            pltpu.VMEM((fit_rows, width), f32),
            pltpu.VMEM((fit_rows, width), f32),
            pltpu.VMEM((2, 2, 2, wide_rows + EDGE, LANES), f32),
            pltpu.VMEM((2, 2, fit_rows, HALF), bf16),
            pltpu.VMEM((2, 2, 2, wide_rows + EDGE, LANES), f32),
            pltpu.VMEM((2, 2, 2, wide_rows + EDGE, LANES), f32),
            dma,
            dma((len(tables) + 1,)),
        ]
        + [dma((len(STEPS),))] * 4
        + [dma((26,))] * 2
        + [dma((4,))] * 2,
        compiler_params=pltpu.CompilerParams(
            collective_id=0, has_side_effects=True, vmem_limit_bytes=50 * 1024 * 1024
        ),
    )(*(pltpu.with_memory_space_constraint(operand, pltpu.HBM) for operand in operands))
    return sharpened[:, None]


def solution(mesh):
    tiles = ("sec", "tile")
    table = P(tiles, None)
    return jax.shard_map(
        functools.partial(local, mesh.shape["sec"], mesh.shape["tile"]),
        mesh=mesh,
        in_specs=(P(tiles, None, None), P(None, tiles, None, None)) + (table,) * 8,
        out_specs=P(None, tiles, None, None),
        check_vma=False,
    )
```

```python
import functools

import jax
import jax.numpy as jnp
from jax import lax
from jax.experimental import pallas as pl
from jax.experimental.pallas import tpu as pltpu
from jax.sharding import PartitionSpec as P

HALO = 32
MHALO = 8
RADIUS = 8
EPSILON = 0.1
GRID_COLS = 4
EDGE = 2 * RADIUS
LANES = 128
HALF = 256
GROUPS = 8
NOWHERE = -1000
TOGETHER = 4
MESH = pl.DeviceIdType.MESH

STEPS = ((1, 0), (-1, 0), (0, 1), (0, -1), (1, 1), (1, -1), (-1, 1), (-1, -1))


def cubic_weights(fraction):
    squared = fraction * fraction
    cubed = squared * fraction
    return (
        -0.5 * cubed + squared - 0.5 * fraction,
        1.5 * cubed - 2.5 * squared + 1.0,
        -1.5 * cubed + 2.0 * squared + 0.5 * fraction,
        0.5 * cubed - 0.5 * squared,
    )


def band(taps, fraction, length, shift):
    line = lax.broadcasted_iota(jnp.int32, (length, taps.shape[1]), 0)
    return band_at(line - shift, taps, fraction)


def band_at(position, taps, fraction):
    weights = cubic_weights(fraction)
    distance = position - taps
    matrix = jnp.zeros(position.shape, jnp.float32)
    for offset in range(4):
        matrix = jnp.where(distance == offset, weights[offset], matrix)
    return matrix.astype(jnp.bfloat16)


def columns(values):
    flat = values.astype(jnp.float32)
    return jnp.transpose(jnp.broadcast_to(flat, (LANES, flat.shape[1])))


def row_bands(positions, taps, fraction):
    taps = columns(taps).astype(jnp.int32)
    weights = [columns(weight) for weight in cubic_weights(fraction)]
    matrices = []
    for position in positions:
        matrix = jnp.zeros(taps.shape, jnp.float32)
        for offset in range(4):
            matrix = jnp.where(position - taps == offset, weights[offset], matrix)
        matrices.append(matrix.astype(jnp.bfloat16))
    return matrices


def spread(values, fill):
    lane = lax.broadcasted_iota(jnp.int32, (1, 2 * HALF), 1)
    both = jnp.concatenate([values[:, :HALF], values[:, values.shape[1] - HALF :]], axis=1)
    return jnp.where((lane >= HALF - EDGE) & (lane < HALF + EDGE), fill, both).astype(values.dtype)


def picker(shape, shift, low, high):
    source = lax.broadcasted_iota(jnp.int32, shape, 0)
    target = lax.broadcasted_iota(jnp.int32, shape, 1)
    chosen = (target - source == shift) & (source >= low) & (source < high)
    return jnp.where(chosen, 1.0, 0.0).astype(jnp.bfloat16)


def dot(left, right):
    return jnp.dot(left, right, preferred_element_type=jnp.float32)


def place(sec_count, tile_count):
    total = sec_count * tile_count
    me = lax.axis_index("sec") * tile_count + lax.axis_index("tile")
    return lax.rem(me + 2, total), total


def resample_kernel(
    sec_count,
    tile_count,
    pan,
    ms,
    row_tap,
    row_frac,
    col_tap,
    col_frac,
    ms_row_tap,
    ms_row_frac,
    ms_col_tap,
    ms_col_frac,
    out,
    wide,
    ms_own,
    row_tap_here,
    row_frac_here,
    col_tap_here,
    col_frac_here,
    ms_row_tap_here,
    ms_row_frac_here,
    ms_col_tap_here,
    ms_col_frac_here,
    far_tap,
    far_frac,
    seg_edge,
    seg_got,
    side_edge,
    side_got,
    pan_patch,
    ms_vert,
    ms_tall,
    pan_pack,
    pan_got,
    ms_pack,
    ms_got,
    corner_pack,
    corner_got,
    packs_pan,
    packs_ms,
    gots_pan,
    gots_ms,
    cmat,
    amat,
    bmat,
    inverse,
    inverse_out,
    own_guide,
    mean_guide,
    inverse_var,
    sums,
    fit,
    pairs,
    fours,
    local_sem,
    table_sem,
    send_pan,
    recv_pan,
    send_ms,
    recv_ms,
    send_tall,
    recv_tall,
    send_table,
    recv_table,
):
    rows, cols = pan.shape
    bands, ms_rows, ms_cols = ms.shape
    placed, total = place(sec_count, tile_count)
    column = lax.rem(placed, GRID_COLS)
    grid_row = placed // GRID_COLS
    north_ok = grid_row > 0
    south_ok = grid_row < total // GRID_COLS - 1
    west_ok = column > 0
    east_ok = column < GRID_COLS - 1

    def device(down, right):
        there = lax.rem(placed + down * GRID_COLS + right - 2 + 2 * total, total)
        return (there // tile_count, lax.rem(there, tile_count))

    def reaches(down, right):
        ok = True
        if down:
            ok = south_ok if down > 0 else north_ok
        if right:
            side = east_ok if right > 0 else west_ok
            ok = side if ok is True else ok & side
        return ok

    def start_all(steps, copies):
        for (down, right), copy in zip(steps, copies):
            pl.when(reaches(down, right))(copy.start)

    def wait_all(steps, copies):
        for (down, right), copy in zip(steps, copies):
            pl.when(reaches(-down, -right))(copy.wait_recv)
        for (down, right), copy in zip(steps, copies):
            pl.when(reaches(down, right))(copy.wait_send)

    barrier = pltpu.get_barrier_semaphore()
    for down, right in STEPS:

        @pl.when(reaches(down, right))
        def _(down=down, right=right):
            pl.semaphore_signal(
                barrier, inc=1, device_id=device(down, right), device_id_type=MESH
            )

    own_copy = pltpu.make_async_copy(
        pan, pan_patch.at[HALO : HALO + rows, LANES : LANES + cols], local_sem
    )
    fetched = [
        pltpu.make_async_copy(source, target, table_sem.at[index])
        for index, (source, target) in enumerate(
            (
                (row_tap, row_tap_here),
                (row_frac, row_frac_here),
                (col_tap, col_tap_here),
                (col_frac, col_frac_here),
                (ms_row_tap, ms_row_tap_here),
                (ms_row_frac, ms_row_frac_here),
                (ms_col_tap, ms_col_tap_here),
                (ms_col_frac, ms_col_frac_here),
                (ms, ms_own),
            )
        )
    ]
    for copy in fetched:
        copy.start()
    own_copy.start()
    group = rows // (LANES // HALO)
    ms_slot = LANES // 2
    folds = range(LANES // HALO)
    pan_movers, ms_movers = [], []
    for side in range(2):
        first_lane = 0 if side else LANES - HALO
        pan_movers.append(
            [
                picker((LANES, LANES), g * HALO - first_lane, first_lane, first_lane + HALO)
                for g in folds
            ]
        )
        first_lane = 0 if side else ms_cols - MHALO
        ms_movers.append(
            [
                picker(
                    (ms_cols, LANES),
                    side * ms_slot + b * MHALO - first_lane,
                    first_lane,
                    first_lane + MHALO,
                )
                for b in range(bands)
            ]
        )

    tall = 1 + north_ok.astype(jnp.int32) + south_ok.astype(jnp.int32)
    broad = 1 + west_ok.astype(jnp.int32) + east_ok.astype(jnp.int32)
    pl.semaphore_wait(barrier, tall * broad - 1)

    def span(step, size, depth):
        if step > 0:
            return slice(size - depth, size), slice(0, depth)
        if step < 0:
            return slice(0, depth), slice(depth + size, 2 * depth + size)
        return slice(0, size), slice(depth, depth + size)

    steps, copies = [], []

    def send_source(index, source, target, send_sems, recv_sems):
        step = STEPS[index]
        copy = pltpu.make_async_remote_copy(
            src_ref=source,
            dst_ref=target,
            send_sem=send_sems.at[index],
            recv_sem=recv_sems.at[index],
            device_id=device(*step),
            device_id_type=MESH,
        )
        steps.append(step)
        copies.append(copy)
        start_all([step], [copy])

    for index, (down, right) in enumerate(STEPS):
        row_from, row_to = span(down, rows, HALO)
        col_from, col_to = span(right, cols, LANES)
        if not right:
            source, target = pan.at[row_from, col_from], pan_patch.at[row_to, col_to]
            send_source(index, source, target, send_pan, recv_pan)
    for copy in fetched:
        copy.wait()
    edge_ms = []
    for side in range(2):
        total_ms = jnp.zeros((ms_rows, LANES), jnp.float32)
        for b in range(bands):
            total_ms = total_ms + dot(ms_own[b], ms_movers[side][b])
        ms_pack[side] = total_ms.astype(jnp.bfloat16)
        edge_ms.append(total_ms)
        lines = slice(0, MHALO) if side else slice(ms_rows - MHALO, ms_rows)
        for pair in range(bands // 2):
            both = [ms_own[b].astype(jnp.float32)[lines] for b in (2 * pair, 2 * pair + 1)]
            ms_tall[side, pair] = jnp.concatenate(both, axis=0).astype(jnp.bfloat16)
    for index, (down, right) in enumerate(STEPS):
        side = 0 if right > 0 else 1
        row_from, row_to = span(down, ms_rows, 16)
        if down and right:
            continue
        if right:
            source, target = ms_pack.at[side, row_from, :], ms_got.at[side, row_to, :]
        else:
            source, target = ms_tall.at[0 if down > 0 else 1], ms_vert.at[0 if down > 0 else 1]
        send_source(index, source, target, send_ms, recv_ms)
    own_copy.wait()
    for side in range(2):
        block = slice(LANES, 2 * LANES) if side else slice(cols, cols + LANES)
        total_pan = jnp.zeros((group, LANES), jnp.float32)
        for g in folds:
            lines = slice(HALO + g * group, HALO + (g + 1) * group)
            total_pan = total_pan + dot(pan_patch[lines, block], pan_movers[side][g])
        pan_pack[side] = total_pan.astype(jnp.bfloat16)
    for index, (down, right) in enumerate(STEPS):
        if not down:
            side = 0 if right > 0 else 1
            send_source(index, pan_pack.at[side], pan_got.at[side], send_pan, recv_pan)
    corners = [(index, step) for index, step in enumerate(STEPS) if step[0] and step[1]]
    for spot, (index, (down, right)) in enumerate(corners):
        side = 0 if right > 0 else 1
        block = slice(LANES, 2 * LANES) if side else slice(cols, cols + LANES)
        first = HALO + (rows - HALO if down > 0 else 0)
        lines = pan_patch[first : first + HALO, block].astype(jnp.float32)
        dense = jnp.zeros((MHALO, LANES), jnp.float32)
        for g in folds:
            part = lines[g * MHALO : (g + 1) * MHALO].astype(jnp.bfloat16)
            dense = dense + dot(part, pan_movers[side][g])
        part = edge_ms[side][ms_rows - MHALO :] if down > 0 else edge_ms[side][:MHALO]
        corner_pack[spot] = jnp.concatenate([dense, part], axis=0).astype(jnp.bfloat16)
        send_source(index, corner_pack.at[spot], corner_got.at[spot], send_pan, recv_pan)
    for index, down in enumerate((1, -1)):
        for which, (source, target) in enumerate(((ms_col_tap, far_tap), (ms_col_frac, far_frac))):
            copy = pltpu.make_async_remote_copy(
                src_ref=source,
                dst_ref=target.at[index],
                send_sem=send_table.at[2 * index + which],
                recv_sem=recv_table.at[2 * index + which],
                device_id=device(down, 0),
                device_id_type=MESH,
            )
            steps.append((down, 0))
            copies.append(copy)
            start_all(steps[-1:], copies[-1:])
    lane = lax.broadcasted_iota(jnp.int32, (rows, LANES), 1)
    patch_rows = 2 * HALO + rows
    row_matrix = jnp.concatenate(
        row_bands(
            [lane + at for at in range(0, patch_rows, LANES)], row_tap_here[...], row_frac_here[...]
        ),
        axis=1,
    )[:, :patch_rows]
    col_matrix = band(
        spread(col_tap_here[...], NOWHERE), spread(col_frac_here[...], 0), 2 * LANES + cols, LANES - HALO
    )
    line = lane
    below = 16 + ms_rows
    away = -LANES
    first_of_pair = jnp.where(
        line < MHALO, line, jnp.where((line < 16) | (line >= below + MHALO), away, line - MHALO)
    )
    second_of_pair = jnp.where(
        line < MHALO,
        away,
        jnp.where(
            line < below, line - MHALO, jnp.where(line < below + MHALO, away, line - 2 * MHALO)
        ),
    )
    ms_row_matrix, *ms_pair_matrices = [
        matrix[:, : 32 + ms_rows]
        for matrix in row_bands(
            [line - (16 - MHALO), first_of_pair, second_of_pair],
            ms_row_tap_here[...],
            ms_row_frac_here[...],
        )
    ]
    def ms_col_matrices(taps, fracs):
        taps, fracs = spread(taps, NOWHERE), spread(fracs, 0)
        lane = lax.broadcasted_iota(jnp.int32, (LANES, taps.shape[1]), 0)
        position = jnp.where(lane < ms_slot, 0, ms_cols + MHALO) + (lane & (MHALO - 1))
        return band(taps, fracs, ms_cols, -MHALO), band_at(position, taps, fracs)

    ms_own_matrix, ms_halo_matrix = ms_col_matrices(ms_col_tap_here[...], ms_col_frac_here[...])
    packers = []
    for shift in (LANES - EDGE, 0):
        line = lax.broadcasted_iota(jnp.int32, (GROUPS * LANES, LANES), 0)
        lane = lax.broadcasted_iota(jnp.int32, (GROUPS * LANES, LANES), 1)
        place_in = (line & (LANES - 1)) - shift
        good = (place_in >= 0) & (place_in < EDGE) & (lane == (line // LANES) * EDGE + place_in)
        packers.append(jnp.where(good, 1.0, 0.0).astype(jnp.bfloat16))

    backs = []
    for side in range(2):
        first_lane = 0 if side else LANES - HALO
        backs.append(
            [
                picker((LANES, LANES), first_lane - g * HALO, g * HALO, (g + 1) * HALO)
                for g in folds
            ]
        )
    wait_all(steps, copies)

    def clear(ok, ref):
        @pl.when(jnp.logical_not(ok))
        def _():
            ref[...] = jnp.zeros(ref.shape, ref.dtype)

    clear(west_ok, pan_got.at[0])
    clear(east_ok, pan_got.at[1])
    for side in range(2):
        block = slice(LANES + cols, 2 * LANES + cols) if side else slice(0, LANES)
        for g in folds:
            lines = slice(HALO + g * group, HALO + (g + 1) * group)
            pan_patch[lines, block] = dot(pan_got[side], backs[side][g]).astype(jnp.bfloat16)

    for spot, (index, (down, right)) in enumerate(corners):
        side = 0 if right > 0 else 1
        block = slice(LANES + cols, 2 * LANES + cols) if side else slice(0, LANES)
        first = 0 if down > 0 else HALO + rows
        parts = [dot(corner_got[spot], backs[side][g])[:MHALO] for g in folds]
        pan_patch[first : first + HALO, block] = jnp.concatenate(parts, axis=0).astype(jnp.bfloat16)
        part = corner_got[spot].astype(jnp.float32)[MHALO:]
        blank = jnp.zeros(part.shape, jnp.float32)
        part = jnp.concatenate([blank, part] if down > 0 else [part, blank], axis=0)
        first = 0 if down > 0 else 16 + ms_rows
        ms_got[side, first : first + 16] = part.astype(jnp.bfloat16)
    clear(north_ok, pan_patch.at[:HALO, :])
    clear(south_ok, pan_patch.at[HALO + rows :, :])
    clear(west_ok, pan_patch.at[:, :LANES])
    clear(east_ok, pan_patch.at[:, LANES + cols :])
    clear(north_ok, ms_vert.at[0])
    clear(south_ok, ms_vert.at[1])
    for side, ok in ((0, west_ok), (1, east_ok)):
        clear(ok, ms_got.at[side])
        clear(north_ok, ms_got.at[side, :16, :])
        clear(south_ok, ms_got.at[side, 16 + ms_rows :, :])

    groups = []

    def send(down, right, source, target):
        index = sum(len(group) for group in groups)
        copy = pltpu.make_async_remote_copy(
            src_ref=source,
            dst_ref=target,
            send_sem=send_tall.at[index],
            recv_sem=recv_tall.at[index],
            device_id=device(down, right),
            device_id_type=MESH,
        )
        groups[-1].append(((down, right), copy))
        start_all([(down, right)], [copy])

    mid = slice(EDGE, EDGE + rows)
    ends = (slice(rows - EDGE, rows), slice(0, EDGE))
    edge_blocks = (slice(2 * HALF - LANES, 2 * HALF), slice(0, LANES))

    def send_sides(channels, packs, gots):
        folds = GROUPS // len(channels)
        depth = rows // folds
        for side, right in ((0, 1), (1, -1)):
            fields = [
                wide[c, EDGE + f * depth : EDGE + (f + 1) * depth, edge_blocks[side]]
                for f in range(folds)
                for c in channels
            ]
            pack, got = packs.at[side], gots.at[side]
            pack[...] = dot(jnp.concatenate(fields, axis=1), packers[side]).astype(jnp.bfloat16)
            send(0, right, pack, got.at[:depth])
            send(1, right, pack.at[depth - EDGE :], got.at[depth : depth + EDGE])
            send(-1, right, pack.at[:EDGE], got.at[depth + EDGE :])

    def open_sides(channels, gots):
        folds = GROUPS // len(channels)
        depth = rows // folds
        count = len(channels)
        for side, ok, block in (
            (0, west_ok, slice(HALF - LANES, HALF)),
            (1, east_ok, slice(HALF, HALF + LANES)),
        ):
            got = gots.at[side]
            clear(ok, got)
            clear(north_ok, got.at[depth : depth + EDGE])
            clear(south_ok, got.at[depth + EDGE :])
            fields = dot(got[...], openers[side]).astype(jnp.bfloat16)
            for index, c in enumerate(channels):
                part = lambda f: fields[:, (f * count + index) * LANES : (f * count + index + 1) * LANES]
                for f in range(folds):
                    wide[c, EDGE + f * depth : EDGE + (f + 1) * depth, block] += part(f)[:depth]
                wide[c, :EDGE, block] += part(folds - 1)[depth : depth + EDGE]
                wide[c, EDGE + rows :, block] += part(0)[depth + EDGE :]

    def wait_group(group):
        wait_all([step for step, _ in group], [copy for _, copy in group])

    groups.append([])
    segment = dot(row_matrix, pan_patch[...]).astype(jnp.bfloat16)
    wide[0, mid, :] = dot(segment, col_matrix).astype(jnp.bfloat16)
    send(1, 0, wide.at[0, rows : rows + EDGE], wide.at[0, :EDGE])
    send(-1, 0, wide.at[0, EDGE : 2 * EDGE], wide.at[0, EDGE + rows :])
    send_sides((0,), packs_pan, gots_pan)
    lane = lax.broadcasted_iota(jnp.int32, (rows, LANES), 1)
    halo_segment = dot(ms_row_matrix, ms_got[0]) + dot(ms_row_matrix, ms_got[1])
    halo_band = (lane & (ms_slot - 1)) // MHALO
    per_group = bands // 2
    for group in range(2):
        groups.append([])
        if group == 0:
            for end in range(2):
                side_edge[end] = halo_segment[ends[end]].astype(jnp.bfloat16)
                send(1 - 2 * end, 0, side_edge.at[end], side_got.at[end])
        members = range(group * per_group, (group + 1) * per_group)
        for b in members:
            block = jnp.concatenate([ms_vert[0, b // 2], ms_own[b], ms_vert[1, b // 2]], axis=0)
            segment = dot(ms_pair_matrices[b % 2], block).astype(jnp.bfloat16)
            for end in range(2):
                seg_edge[end, b] = segment[ends[end]]
            beside = jnp.where(halo_band == b, halo_segment, 0.0).astype(jnp.bfloat16)
            wide[b + 1, mid, :] = (
                dot(segment, ms_own_matrix) + dot(beside, ms_halo_matrix)
            ).astype(jnp.bfloat16)
        for end in range(2):
            part = slice(group * per_group, (group + 1) * per_group)
            send(1 - 2 * end, 0, seg_edge.at[end, part], seg_got.at[end, part])
        send_sides(tuple(b + 1 for b in members), packs_ms.at[group], gots_ms.at[group])

    setup(placed, total, rows, cols, wide, cmat, amat, bmat, inverse, inverse_out, own_guide)
    openers = []
    for shift in (LANES - EDGE, 0):
        line = lax.broadcasted_iota(jnp.int32, (LANES, GROUPS * LANES), 0)
        lane = lax.broadcasted_iota(jnp.int32, (LANES, GROUPS * LANES), 1)
        place_in = (lane & (LANES - 1)) - shift
        good = (place_in >= 0) & (place_in < EDGE) & (line == (lane // LANES) * EDGE + place_in)
        openers.append(jnp.where(good, 1.0, 0.0).astype(jnp.bfloat16))
    far_matrices = [ms_col_matrices(far_tap[end], far_frac[end]) for end in range(2)]

    wait_group(groups[0])
    clear(north_ok, wide.at[0, :EDGE])
    clear(south_ok, wide.at[0, EDGE + rows :])
    open_sides((0,), gots_pan)
    guide_stats(
        rows, wide, cmat, inverse, mean_guide, inverse_var, sums.at[0], pairs.at[0], fours.at[0]
    )
    line = lax.broadcasted_iota(jnp.int32, (per_group * EDGE, LANES), 0)
    lane = lax.broadcasted_iota(jnp.int32, (per_group * EDGE, LANES), 1)
    for group in range(2):
        first = group * per_group
        wait_group(groups[group + 1])
        chosen = (lane & (ms_slot - 1)) // MHALO == line // EDGE + first
        for end, lines in ((0, slice(0, EDGE)), (1, slice(EDGE + rows, 2 * EDGE + rows))):
            own_matrix, halo_matrix = far_matrices[end]
            side = jnp.concatenate([side_got[end]] * per_group, axis=0)
            side = jnp.where(chosen, side.astype(jnp.float32), 0.0).astype(jnp.bfloat16)
            piece = seg_got[end, first : first + per_group].reshape(per_group * EDGE, ms_cols)
            far = dot(piece, own_matrix) + dot(side, halo_matrix)
            for b in range(per_group):
                wide[first + b + 1, lines, :] = far[b * EDGE : (b + 1) * EDGE].astype(jnp.bfloat16)
        members = slice(first + 1, first + per_group + 1)
        clear(north_ok, wide.at[members, :EDGE, :])
        clear(south_ok, wide.at[members, EDGE + rows :, :])
        open_sides(tuple(range(first + 1, first + per_group + 1)), gots_ms.at[group])

        def item(index):
            b = first + index
            work = [ref.at[index % TOGETHER] for ref in (sums, fit, pairs, fours)]
            return wide.at[b + 1], out.at[b], work

        stage_dots(rows, wide.at[0], *item(0), cmat)
        stage_dots(rows, wide.at[0], *item(1), cmat)
        stage_fit(rows, *item(0), inverse, mean_guide, inverse_var)
        stage_dots(rows, wide.at[0], *item(2), cmat)
        stage_fit(rows, *item(1), inverse, mean_guide, inverse_var)
        stage_spread(rows, *item(0), amat, bmat)
        stage_dots(rows, wide.at[0], *item(3), cmat)
        stage_fit(rows, *item(2), inverse, mean_guide, inverse_var)
        stage_out(rows, *item(0), inverse_out, own_guide)
        stage_spread(rows, *item(1), amat, bmat)
        stage_fit(rows, *item(3), inverse, mean_guide, inverse_var)
        stage_out(rows, *item(1), inverse_out, own_guide)
        stage_spread(rows, *item(2), amat, bmat)
        stage_out(rows, *item(2), inverse_out, own_guide)
        stage_spread(rows, *item(3), amat, bmat)
        stage_out(rows, *item(3), inverse_out, own_guide)


def sum_down(lines, pairs, fours, kept):
    count = kept + EDGE
    pairs[:count] = lines[:count] + lines[1 : count + 1]
    fours[:count] = pairs[:count] + pairs[2 : count + 2]
    eights = fours[: kept + 8] + fours[4 : kept + 12]
    return eights[:kept] + eights[8:] + lines[EDGE:count]


def inv_cover(places, extent, ok):
    highest = jnp.minimum(places + RADIUS, extent - 1)
    lowest = jnp.maximum(places - RADIUS, 0)
    inside = (places >= 0) & (places < extent) & ok
    cover = jnp.where(inside, highest - lowest + 1, 1).astype(jnp.float32)
    return jnp.where(inside, 1.0 / cover, 0.0)

def sum_down(lines, pairs, fours, kept):
    count = kept + EDGE
    pairs[:count] = lines[:count] + lines[1 : count + 1]
    fours[:count] = pairs[:count] + pairs[2 : count + 2]
    eights = fours[: kept + 8] + fours[4 : kept + 12]
    return eights[:kept] + eights[8:] + lines[EDGE:count]


def setup(placed, total, rows, cols, guide, cmat, amat, bmat, inverse, inverse_out, own):
    fit_rows = rows + EDGE
    column = lax.rem(placed, GRID_COLS)
    grid_row = placed // GRID_COLS
    map_rows = total // GRID_COLS * rows
    map_cols = GRID_COLS * cols
    k = lax.broadcasted_iota(jnp.int32, (HALF, HALF), 0)
    j = lax.broadcasted_iota(jnp.int32, (HALF, HALF), 1)
    cmat[...] = jnp.where(((j - k + 2 * HALF) & (HALF - 1)) <= EDGE, 1.0, 0.0).astype(jnp.bfloat16)
    k = lax.broadcasted_iota(jnp.int32, (HALF, HALF), 0)
    j = lax.broadcasted_iota(jnp.int32, (HALF, HALF), 1)
    first_b = HALF - EDGE - EDGE
    amat[...] = jnp.where((k >= j) & (k - j <= EDGE) & (j < first_b), 1.0, 0.0).astype(jnp.bfloat16)
    off = cols - HALF
    fit_at = jnp.where(k < EDGE, HALF, 0) + k - RADIUS
    bmat[...] = jnp.where((jnp.abs(fit_at - j) <= RADIUS) & (j >= first_b - off) & ((k < EDGE) | (k >= 2 * EDGE)), 1.0, 0.0).astype(jnp.bfloat16)
    row0 = grid_row * rows
    col0 = column * cols
    lane = lax.broadcasted_iota(jnp.int32, (1, 2 * HALF), 1)
    in_b = lane >= HALF
    i = lane - HALF
    fit_col = jnp.where(in_b, jnp.where(i < EDGE, cols, off) + i - RADIUS, lane - RADIUS)
    ok = (lane < HALF - EDGE) | (in_b & ((i < EDGE) | (i >= 2 * EDGE)))
    line = lax.broadcasted_iota(jnp.int32, (fit_rows, 1), 0)
    inverse[...] = inv_cover(row0 - RADIUS + line, map_rows, line >= 0) * inv_cover(col0 + fit_col, map_cols, ok)
    line = lax.broadcasted_iota(jnp.int32, (rows, 1), 0)
    lane = lax.broadcasted_iota(jnp.int32, (1, cols), 1)
    inverse_out[...] = inv_cover(row0 + line, map_rows, line >= 0) * inv_cover(col0 + lane, map_cols, lane >= 0)
    mid = slice(EDGE, EDGE + rows)
    own[:, :LANES] = guide[0, mid, :LANES].astype(jnp.float32)
    l = lax.broadcasted_iota(jnp.int32, (rows, LANES), 1)
    own[:, LANES:2*LANES] = jnp.where(l < LANES // 2, guide[0, mid, LANES:2*LANES].astype(jnp.float32), guide[0, mid, HALF:HALF+LANES].astype(jnp.float32))
    own[:, 2*LANES:] = guide[0, mid, HALF + LANES:].astype(jnp.float32)

def split_dot(values, cmat):
    high = values.astype(jnp.bfloat16)
    low = (values - high.astype(jnp.float32)).astype(jnp.bfloat16)
    return dot(high, cmat[...]) + dot(low, cmat[...])

def put(target, values):
    for t in range(2):
        target[t, : values.shape[0]] = values[:, t * LANES : (t + 1) * LANES]

def guide_stats(rows, guide, cmat, inverse, mean_guide, inverse_var, sums, pairs, fours):
    fit_rows = rows + EDGE
    for h in range(2):
        half = slice(h * HALF, (h + 1) * HALF)
        g = guide[0, :, half]
        gf = g.astype(jnp.float32)
        put(sums.at[h, 0], dot(g, cmat[...]))
        put(sums.at[h, 1], split_dot(gf * gf, cmat))
        for t in range(2):
            lanes = slice(h * HALF + t * LANES, h * HALF + (t + 1) * LANES)
            scale = inverse[:, lanes]
            mean = sum_down(sums.at[h, 0, t], pairs.at[h, 0, t], fours.at[h, 0, t], fit_rows) * scale
            square = sum_down(sums.at[h, 1, t], pairs.at[h, 1, t], fours.at[h, 1, t], fit_rows) * scale
            mean_guide[:, lanes] = mean
            inverse_var[:, lanes] = 1.0 / (square - mean * mean + EPSILON)


def stage_dots(rows, guide, bandref, out, work, cmat):
    sums, fit, pairs, fours = work
    fit_rows = rows + EDGE
    for h in range(2):
        half = slice(h * HALF, (h + 1) * HALF)
        p = bandref[:, half]
        put(sums.at[h, 0], dot(p, cmat[...]))
        put(sums.at[h, 1], split_dot(guide[:, half].astype(jnp.float32) * p.astype(jnp.float32), cmat))


def stage_fit(rows, bandref, out, work, inverse, mean_guide, inverse_var):
    sums, fit, pairs, fours = work
    fit_rows = rows + EDGE
    for h in range(2):
        for t in range(2):
            lanes = slice(h * HALF + t * LANES, h * HALF + (t + 1) * LANES)
            scale = inverse[:, lanes]
            mean = mean_guide[:, lanes]
            mean_band = sum_down(sums.at[h, 0, t], pairs.at[h, 0, t], fours.at[h, 0, t], fit_rows) * scale
            cross = sum_down(sums.at[h, 1, t], pairs.at[h, 1, t], fours.at[h, 1, t], fit_rows) * scale
            gain = (cross - mean * mean_band) * inverse_var[:, lanes]
            fit[h, 0, :, t * LANES : (t + 1) * LANES] = gain.astype(jnp.bfloat16)
            fit[h, 1, :, t * LANES : (t + 1) * LANES] = (mean_band - gain * mean).astype(jnp.bfloat16)


def stage_spread(rows, bandref, out, work, amat, bmat):
    sums, fit, pairs, fours = work
    fit_rows = rows + EDGE
    for q in range(2):
        a = dot(fit[0, q], amat[...])
        b = dot(fit[1, q], bmat[...])
        sums[0, q, 0, :fit_rows] = a[:, :LANES]
        sums[0, q, 1, :fit_rows] = a[:, LANES:] + b[:, :LANES]
        sums[1, q, 0, :fit_rows] = b[:, LANES:]


def stage_out(rows, bandref, out, work, inverse_out, own):
    sums, fit, pairs, fours = work
    fit_rows = rows + EDGE
    for t in range(3):
        lanes = slice(t * LANES, (t + 1) * LANES)
        gain = sum_down(sums.at[t // 2, 0, t % 2], pairs.at[t // 2, 0, t % 2], fours.at[t // 2, 0, t % 2], rows)
        offset = sum_down(sums.at[t // 2, 1, t % 2], pairs.at[t // 2, 1, t % 2], fours.at[t // 2, 1, t % 2], rows)
        out[:, lanes] = ((gain * own[:, lanes] + offset) * inverse_out[:, lanes]).astype(jnp.bfloat16)


def local(sec_count, tile_count, pan_source, ms_source, *tables):
    rows, cols = pan_source.shape[1:]
    bands, _, ms_rows, ms_cols = ms_source.shape
    channels = bands + 1
    wide_rows = rows + 2 * EDGE
    width = 2 * HALF
    dense_rows = rows + rows // GROUPS
    fit_rows = rows + EDGE
    depth = rows // GROUPS
    half_bands = bands // 2
    fold_rows = rows * half_bands // GROUPS
    bf16, f32 = jnp.bfloat16, jnp.float32
    dma = pltpu.SemaphoreType.DMA
    hbm = pl.BlockSpec(memory_space=pltpu.HBM)
    operands = (pan_source.reshape(rows, cols), ms_source.reshape(bands, ms_rows, ms_cols)) + tables
    sharpened = pl.pallas_call(
        functools.partial(resample_kernel, sec_count, tile_count),
        out_shape=pltpu.VMEM((bands, rows, cols), bf16),
        in_specs=[hbm] * (2 + len(tables)),
        out_specs=pl.BlockSpec(memory_space=pltpu.VMEM),
        scratch_shapes=[
            pltpu.VMEM((channels, wide_rows, width), bf16),
            pltpu.VMEM((bands, ms_rows, ms_cols), bf16),
        ]
        + [pltpu.VMEM(table.shape, table.dtype) for table in tables]
        + [
            pltpu.VMEM((2,) + tables[6].shape, tables[6].dtype),
            pltpu.VMEM((2,) + tables[7].shape, tables[7].dtype),
            pltpu.VMEM((2, bands, EDGE, ms_cols), bf16),
            pltpu.VMEM((2, bands, EDGE, ms_cols), bf16),
            pltpu.VMEM((2, EDGE, LANES), bf16),
            pltpu.VMEM((2, EDGE, LANES), bf16),
            pltpu.VMEM((rows + 2 * HALO, cols + 2 * LANES), bf16),
            pltpu.VMEM((2, bands // 2, 16, ms_cols), bf16),
            pltpu.VMEM((2, bands // 2, 16, ms_cols), bf16),
            pltpu.VMEM((2, rows * HALO // LANES, LANES), bf16),
            pltpu.VMEM((2, rows * HALO // LANES, LANES), bf16),
            pltpu.VMEM((2, ms_rows, LANES), bf16),
            pltpu.VMEM((2, ms_rows + 32, LANES), bf16),
            pltpu.VMEM((4, 16, LANES), bf16),
            pltpu.VMEM((4, 16, LANES), bf16),
            pltpu.VMEM((2, depth, LANES), bf16),
            pltpu.VMEM((2, 2, fold_rows, LANES), bf16),
            pltpu.VMEM((2, depth + 2 * EDGE, LANES), bf16),
            pltpu.VMEM((2, 2, fold_rows + 2 * EDGE, LANES), bf16),
            pltpu.VMEM((HALF, HALF), bf16),
            pltpu.VMEM((HALF, HALF), bf16),
            pltpu.VMEM((HALF, HALF), bf16),
            pltpu.VMEM((fit_rows, width), f32),
            pltpu.VMEM((rows, cols), f32),
            pltpu.VMEM((rows, cols), f32),
            pltpu.VMEM((fit_rows, width), f32),
            pltpu.VMEM((fit_rows, width), f32),
            pltpu.VMEM((TOGETHER, 2, 2, 2, wide_rows + EDGE, LANES), f32),
            pltpu.VMEM((TOGETHER, 2, 2, fit_rows, HALF), bf16),
            pltpu.VMEM((TOGETHER, 2, 2, 2, wide_rows + EDGE, LANES), f32),
            pltpu.VMEM((TOGETHER, 2, 2, 2, wide_rows + EDGE, LANES), f32),
            dma,
            dma((len(tables) + 1,)),
        ]
        + [dma((len(STEPS),))] * 4
        + [dma((26,))] * 2
        + [dma((4,))] * 2,
        compiler_params=pltpu.CompilerParams(
            collective_id=0, has_side_effects=True, vmem_limit_bytes=50 * 1024 * 1024
        ),
    )(*(pltpu.with_memory_space_constraint(operand, pltpu.HBM) for operand in operands))
    return sharpened[:, None]


def solution(mesh):
    tiles = ("sec", "tile")
    table = P(tiles, None)
    return jax.shard_map(
        functools.partial(local, mesh.shape["sec"], mesh.shape["tile"]),
        mesh=mesh,
        in_specs=(P(tiles, None, None), P(None, tiles, None, None)) + (table,) * 8,
        out_specs=P(None, tiles, None, None),
        check_vma=False,
    )
```
